256 devices in a mesh: head: 8 (over z), tok: 32 (over x, y, core).
Axes of the slice: x: 4, y: 4, z: 8, core: 2. Of those that a mesh axis runs over, the one named last changes fastest.
Arguments:
- video_q: bfloat16 [28672, 2048], P('tok', 'head'), may hold values from -6 to 6
- video_k: bfloat16 [28672, 2048], P('tok', 'head'), may hold values from -6 to 6
- video_v: bfloat16 [28672, 2048], P('tok', 'head'), may hold values from -6 to 6
- audio_q: bfloat16 [1024, 2048], P('tok', 'head'), may hold values from -6 to 6
- audio_k: bfloat16 [1024, 2048], P('tok', 'head'), may hold values from -6 to 6
- audio_v: bfloat16 [1024, 2048], P('tok', 'head'), may hold values from -6 to 6
- norm_gain: float32 [2048], replicated, may hold values from 0.5 to 1.5
Outputs:
- video_out: bfloat16 [28672, 2048], P(('tok', 'head'))
- audio_out: bfloat16 [1024, 2048], P('tok', 'head')
The draws below stay inside these ranges and needn't reach their ends.
All inputs are finite; a program needn't handle non-finite values.
Results may differ from the reference program's by a relative error of at most 0.0095.
Values may be sent and summed in bfloat16 or wider, within the bound.
A program may use at most 64 MiB of HBM per device.

```python
import jax
import jax.numpy as jnp
from jax import lax

HEADS = 32
HEAD_DIM = 64
D = 2048
VTOK = 28672
ATOK = 1024


def base_draw(key, salt, count):
    sub = jax.random.fold_in(key, salt)
    return jnp.clip(jax.random.normal(sub, (count, D), jnp.float32), -6.0, 6.0)


def query_draw(key, salt, count):
    values = base_draw(key, salt, count)
    return values


def key_draw(key, salt, count):
    values = base_draw(key, salt, count)
    return values


def draw_video_q(key, part):
    return query_draw(key, 11, VTOK).astype(jnp.bfloat16)


def draw_video_k(key, part):
    return key_draw(key, 12, VTOK).astype(jnp.bfloat16)


def draw_audio_q(key, part):
    return query_draw(key, 13, ATOK).astype(jnp.bfloat16)


def draw_audio_k(key, part):
    return key_draw(key, 14, ATOK).astype(jnp.bfloat16)


def level_of(rng, shape, pieces, low, top_value):
    loudness, own = 1.0, jax.random.fold_in(rng, 6)
    for position, parts in pieces:
        draws = jnp.exp(jax.random.uniform(jax.random.fold_in(own, position), (parts,), jnp.float32, low / len(pieces), top_value / len(pieces)))
        loudness = loudness * jnp.repeat(draws, shape[position] // parts).reshape([-1 if axis == position else 1 for axis in range(len(shape))])
    return loudness


def gaussian(key, dims, deviation, most, shards=(), held_as=jnp.bfloat16):
    factor_of = level_of(key, dims, shards, -0.22, 0.18) if shards else 1.0
    values = jax.random.normal(key, dims, jnp.float32) * deviation * factor_of
    return jnp.minimum(jnp.maximum(values, -most), most).astype(held_as)


def setup_inputs(seed: int = 0) -> dict:
    arg_keys = jax.random.split(jax.random.key(seed), 8)
    video_q = draw_video_q(jax.random.fold_in(arg_keys[7], 71), 0)
    video_k = draw_video_k(jax.random.fold_in(arg_keys[7], 71), 0)
    video_v = gaussian(arg_keys[2], (VTOK, D), 1.0, 6.0, ((0, 32), (1, 8)))
    audio_q = draw_audio_q(jax.random.fold_in(arg_keys[7], 71), 0)
    audio_k = draw_audio_k(jax.random.fold_in(arg_keys[7], 71), 0)
    audio_v = gaussian(arg_keys[5], (ATOK, D), 1.0, 6.0, ((0, 32), (1, 8)))
    norm_gain = jnp.clip(1.0 + 0.1 * jax.random.normal(arg_keys[6], (D,), jnp.float32), 0.5, 1.5)
    return dict(video_q=video_q, video_k=video_k, video_v=video_v, audio_q=audio_q, audio_k=audio_k, audio_v=audio_v, norm_gain=norm_gain)


def attend(query_part, key_part, value_part):
    scaling = HEAD_DIM ** (-0.5)

    def split_heads(matrix):
        return matrix.reshape(matrix.shape[0], HEADS, HEAD_DIM).transpose(1, 0, 2)

    def one_head(triple):
        query_head, key_head, value_head = triple
        scores = jnp.dot(query_head, key_head.T, preferred_element_type=jnp.float32) * scaling
        row_max = lax.optimization_barrier(jnp.max(scores, axis=1, keepdims=True))
        weights = jnp.exp(scores - row_max)
        row_sum = lax.optimization_barrier(jnp.sum(weights, axis=1, keepdims=True))
        result = jnp.dot(weights.astype(jnp.bfloat16), value_head, preferred_element_type=jnp.float32) / row_sum
        return result.astype(jnp.bfloat16)
    heads_out = lax.map(one_head, (split_heads(query_part), split_heads(key_part), split_heads(value_part)))
    return heads_out.transpose(1, 0, 2).reshape(query_part.shape[0], HEADS * HEAD_DIM)

def reference(video_q, video_k, video_v, audio_q, audio_k, audio_v, norm_gain):
    video_attn = attend(video_q, audio_k, audio_v)
    widened = video_attn.astype(jnp.float32)
    mean_square = lax.optimization_barrier(jnp.mean(widened * widened, axis=1, keepdims=True))
    video_out = (widened * lax.rsqrt(mean_square + 1e-06) * norm_gain).astype(jnp.bfloat16)
    audio_out = attend(audio_q, video_k, video_v)
    return (video_out, audio_out)
```

```python
import jax
import jax.numpy as jnp
from jax import lax
from jax.experimental import pallas as pl
from jax.experimental.pallas import tpu as pltpu
from jax.sharding import PartitionSpec as P

MESH = pl.DeviceIdType.MESH
F32, BF16 = jnp.float32, jnp.bfloat16
HEAD_DIM = 64
LOG2E = 1.4426950408889634
NZ = 8
NT = 32
ROWS = 896
PIECE = 112
AROWS = 32
WIDTH = 256
KEYS = 1024
AUG = 80


def key_blocks(count):
    starts = list(range(0, count, 256))
    return [(start, min(256, count - start)) for start in starts]


def kernel(vq, vk, vv, aq, ak, av, gain, vout, aout,
           q_buf, k_buf, v_buf, qt, vt_local, kvg, qg, vt_audio, qt_audio,
           s_a, s_b, o_t, stage, recv, ret_stage, ret_recv, stat, stat_recv, w_buf,
           in_sem, kv_send, kv_recv, q_send, q_recv, fwd_send, fwd_recv,
           z_send, z_recv, ret_send, ret_rsem, st_send, st_rsem):
    z = lax.axis_index("head")
    t = lax.axis_index("tok")
    x, y, c = t // 8, (t // 2) % 4, t % 2

    def tok_of(dx, dy, dc):
        return (((x + dx) % 4) * 4 + (y + dy) % 4) * 2 + (c + dc) % 2

    own = [
        pltpu.make_async_copy(ak, kvg.at[0, 0], in_sem.at[0]),
        pltpu.make_async_copy(av, kvg.at[0, 1], in_sem.at[1]),
        pltpu.make_async_copy(aq, qg.at[0], in_sem.at[2]),
        pltpu.make_async_copy(vq, q_buf, in_sem.at[3]),
        pltpu.make_async_copy(vv, v_buf, in_sem.at[4]),
        pltpu.make_async_copy(vk, k_buf, in_sem.at[5]),
    ]
    for copy in own:
        copy.start()

    barrier = pltpu.get_barrier_semaphore()

    def greet_tok(b, carry):
        pl.semaphore_signal(barrier, inc=1, device_id=(z, tok_of(b // 4, b % 4, b // 16)),
                            device_id_type=MESH)
        return carry

    lax.fori_loop(1, NT, greet_tok, 0)

    def greet_head(d, carry):
        pl.semaphore_signal(barrier, inc=1, device_id=((z + d) % NZ, t), device_id_type=MESH)
        return carry

    lax.fori_loop(1, NZ, greet_head, 0)
    for copy in own[:3]:
        copy.wait()
    pl.semaphore_wait(barrier, NT - 1 + NZ - 1)

    def kv_copy(b):
        return pltpu.make_async_remote_copy(
            src_ref=kvg.at[0], dst_ref=kvg.at[b], send_sem=kv_send.at[b], recv_sem=kv_recv.at[b],
            device_id=(z, tok_of(4 - b // 4, 4 - b % 4, 0)), device_id_type=MESH)

    def q_copy(b):
        return pltpu.make_async_remote_copy(
            src_ref=qg.at[0], dst_ref=qg.at[b], send_sem=q_send.at[b], recv_sem=q_recv.at[b],
            device_id=(z, tok_of(4 - b // 4, 4 - b % 4, 0)), device_id_type=MESH)

    def loop(start, stop, body):
        def step(i, carry):
            body(i)
            return carry
        lax.fori_loop(start, stop, step, 0)

    loop(1, 16, lambda b: kv_copy(b).start())
    loop(1, 16, lambda b: q_copy(b).start())

    own[3].wait()
    for j in range(4):
        parts = []
        for d in (j + 1, (NZ - j) % NZ):
            start = pl.multiple_of(((z + d) % NZ) * PIECE, 16)
            parts.append(q_buf[pl.ds(start, PIECE), :])
            parts.append(jnp.zeros((128 - PIECE, WIDTH), BF16))
        qt[j] = jnp.concatenate(parts, axis=0).T * BF16(0.125)
    own[4].wait()
    for h in range(4):
        vt_local[h, HEAD_DIM:, :] = jnp.ones((AUG - HEAD_DIM, ROWS), BF16)
        vt_audio[h, HEAD_DIM:, :] = jnp.ones((AUG - HEAD_DIM, KEYS), BF16)
    for start, size in key_blocks(ROWS):
        turned = v_buf[start:start + size, :].T
        for h in range(4):
            vt_local[h, :HEAD_DIM, start:start + size] = turned[h * HEAD_DIM:(h + 1) * HEAD_DIM]
    own[5].wait()

    loop(1, 16, lambda b: kv_copy(b).wait_recv())
    sibling = (z, tok_of(0, 0, 1))
    kv_fwd = pltpu.make_async_remote_copy(
        src_ref=kvg.at[0:16], dst_ref=kvg.at[16:32], send_sem=fwd_send.at[0],
        recv_sem=fwd_recv.at[0], device_id=sibling, device_id_type=MESH)
    kv_fwd.start()
    q_fwd = pltpu.make_async_remote_copy(
        src_ref=qg.at[0:16], dst_ref=qg.at[16:32], send_sem=fwd_send.at[1],
        recv_sem=fwd_recv.at[1], device_id=sibling, device_id_type=MESH)

    def turn_values(half):
        for kb in (2 * half, 2 * half + 1):
            turned = kvg[8 * kb:8 * kb + 8, 1].reshape(256, WIDTH).T
            for h in range(4):
                vt_audio[h, :HEAD_DIM, kb * 256:kb * 256 + 256] = (
                    turned[h * HEAD_DIM:(h + 1) * HEAD_DIM])

    turn_values(0)
    kv_fwd.wait_recv()
    turn_values(1)

    row = lax.broadcasted_iota(jnp.int32, (128, 256), 0)

    def masked(qt_ref, j, h):
        pair = qt_ref[j, (h // 2) * 128:(h // 2) * 128 + 128, :]
        keep = (row < HEAD_DIM) if h % 2 == 0 else (row >= HEAD_DIM)
        return jnp.where(keep, pair, jnp.zeros_like(pair))

    def audio_keys(start, size, h):
        lanes = slice((h // 2) * 128, (h // 2) * 128 + 128)
        return kvg[start // 32:(start + size) // 32, 0, :, lanes].reshape(size, 128)

    def video_keys(start, size, h):
        return k_buf[start:start + size, (h // 2) * 128:(h // 2) * 128 + 128]

    def both(first, second):
        top, acc = None, None
        if first is not None:
            keys, count, qt_ref, j, h, s_out = first
            q_head = masked(qt_ref, j, h)
        if second is not None:
            s_in, top_in, vt_ref, h_in, count_in = second
        blocks = key_blocks(count if first is not None else count_in)
        for start, size in blocks:
            if first is not None:
                s = jnp.dot(keys(start, size, h), q_head, preferred_element_type=F32)
                s_out[start:start + size, :] = s
                part = jnp.max(s.reshape(size // 8, 8, 256), axis=0)
                top = part if top is None else jnp.maximum(top, part)
            if second is not None:
                w = jnp.exp2((s_in[start:start + size, :] - top_in) * LOG2E).astype(BF16)
                o = jnp.dot(vt_ref[h_in, :, start:start + size], w, preferred_element_type=F32)
                acc = o if acc is None else acc + o
        if top is not None:
            top = jnp.max(top, axis=0, keepdims=True)
        return top, acc

    def z_copy(d, slot):
        return pltpu.make_async_remote_copy(
            src_ref=stage.at[slot], dst_ref=recv.at[d], send_sem=z_send.at[d],
            recv_sem=z_recv.at[d], device_id=((z + d) % NZ, t), device_id_type=MESH)

    def slot_of(d):
        return 2 * (d - 1) if d <= 4 else 2 * (NZ - d) + 1

    def video_chunk(j, top):
        after = jnp.minimum(j + 1, 3)
        steps = [(0, j, s_a), (1, j, s_b), (2, j, s_a), (3, j, s_b), (0, after, s_a)]
        for h in range(4):
            nh, nj, ns = steps[h + 1]
            top, acc = both((audio_keys, KEYS, qt, nj, nh, ns), (steps[h][2], top, vt_audio, h, KEYS))
            o_t[h * HEAD_DIM:(h + 1) * HEAD_DIM, :] = acc[:HEAD_DIM] / acc[HEAD_DIM:HEAD_DIM + 1]
        out = o_t[...].T.astype(BF16)
        stage[2 * j] = out[:PIECE]
        stage[2 * j + 1] = out[128:128 + PIECE]
        z_copy(j + 1, 2 * j).start()

        @pl.when(j > 0)
        def _():
            z_copy(NZ - j, 2 * j + 1).start()

        @pl.when(j == 1)
        def _():
            loop(1, 16, lambda b: q_copy(b).wait_recv())
            q_fwd.start()
        return top

    top, _ = both((audio_keys, KEYS, qt, 0, 0, s_a), None)
    lax.fori_loop(0, 4, video_chunk, top)

    q_fwd.wait_recv()
    for j in range(4):
        qt_audio[j] = qg[8 * j:8 * j + 8].reshape(256, WIDTH).T * BF16(0.125)

    def ret_copies(b, half):
        device = (z, tok_of(b // 4, b % 4, b // 16))
        return (
            pltpu.make_async_remote_copy(
                src_ref=ret_stage.at[b], dst_ref=ret_recv.at[b], send_sem=ret_send.at[b],
                recv_sem=ret_rsem.at[b], device_id=device, device_id_type=MESH),
            pltpu.make_async_remote_copy(
                src_ref=stat.at[b // 8, half], dst_ref=stat_recv.at[b], send_sem=st_send.at[b],
                recv_sem=st_rsem.at[b], device_id=device, device_id_type=MESH))

    def audio_chunk(j, top):
        after = jnp.minimum(j + 1, 3)
        steps = [(0, j, s_a), (1, j, s_b), (2, j, s_a), (3, j, s_b), (0, after, s_a)]
        for h in range(4):
            nh, nj, ns = steps[h + 1]
            top_h = top
            top, acc = both((video_keys, ROWS, qt_audio, nj, nh, ns),
                            (steps[h][2], top_h, vt_local, h, ROWS))
            o_t[h * HEAD_DIM:(h + 1) * HEAD_DIM, :] = acc[:HEAD_DIM]
            for half in range(2):
                lanes = slice(half * 128, half * 128 + 128)
                stat[j, half, h:h + 1, :] = top_h[:, lanes]
                stat[j, half, 4 + h:5 + h, :] = acc[HEAD_DIM:HEAD_DIM + 1, lanes]
        out = o_t[...].T.astype(BF16).reshape(8, AROWS, WIDTH)
        for p in range(8):
            ret_stage[8 * j + p] = out[p]
        for p in range(8):
            def send(b=8 * j + p, half=p // 4):
                for copy in ret_copies(b, half):
                    copy.start()
            if p == 0:
                pl.when(j > 0)(send)
            else:
                send()
        return top

    top, _ = both((video_keys, ROWS, qt_audio, 0, 0, s_a), None)
    lax.fori_loop(0, 4, audio_chunk, top)

    for d in range(1, NZ):
        z_copy(d, slot_of(d)).wait_recv()

    def received(d):
        return (stage[1] if d == 0 else recv[d]).astype(F32)

    total = None
    for d in range(NZ):
        wide = received(d)
        part = jnp.sum(wide * wide, axis=1, keepdims=True)
        total = part if total is None else total + part
    factor = lax.rsqrt(total * (1.0 / (NZ * WIDTH)) + 1e-06)
    for d in range(NZ):
        column = pl.multiple_of(((z + NZ - d) % NZ) * WIDTH, WIDTH)
        lanes = pl.ds(column, WIDTH)
        vout[:, lanes] = (received(d) * factor * gain[:, lanes]).astype(BF16)

    def ret_wait(b):
        for copy in ret_copies(b, (b % 8) // 4):
            copy.wait_recv()

    loop(1, NT, ret_wait)
    tiles = []
    for b in range(NT):
        tile = stat[0, 0] if b == 0 else stat_recv[b]
        shift = (128 - 32 * (b % 4)) % 128
        tiles.append(pltpu.roll(tile, shift, 1) if shift else tile)
    peak = tiles[0]
    for tile in tiles[1:]:
        peak = jnp.maximum(peak, tile)
    norm = None
    weights = []
    for tile in tiles:
        w = jnp.exp2((tile - peak) * LOG2E)
        weights.append(w)
        part = w * pltpu.roll(tile, 4, 0)
        norm = part if norm is None else norm + part
    for b in range(NT):
        w_buf[b] = weights[b] / norm
    turned = w_buf[...].reshape(256, 128).T[:AROWS]
    lane = lax.broadcasted_iota(jnp.int32, (AROWS, 128), 1)
    merged = [None, None]
    for b in range(NT):
        for pair in range(2):
            at = b * 8 + 2 * pair
            w = jnp.where(lane < HEAD_DIM, turned[:, at:at + 1], turned[:, at + 1:at + 2])
            lanes = slice(pair * 128, pair * 128 + 128)
            part = w * (ret_stage[0, :, lanes] if b == 0 else ret_recv[b, :, lanes]).astype(F32)
            merged[pair] = part if merged[pair] is None else merged[pair] + part
    for pair in range(2):
        aout[:, pair * 128:pair * 128 + 128] = merged[pair].astype(BF16)

    def sent_gather(b):
        kv_copy(b).wait_send()
        q_copy(b).wait_send()

    loop(1, 16, sent_gather)
    kv_fwd.wait_send()
    q_fwd.wait_send()
    for d in range(1, NZ):
        z_copy(d, slot_of(d)).wait_send()

    def sent_back(b):
        for copy in ret_copies(b, (b % 8) // 4):
            copy.wait_send()

    loop(1, NT, sent_back)


def shards(video_q, video_k, video_v, audio_q, audio_k, audio_v, norm_gain):
    hbm = pl.BlockSpec(memory_space=pl.ANY)
    vmem = pl.BlockSpec(memory_space=pltpu.VMEM)
    dma = pltpu.SemaphoreType.DMA
    return pl.pallas_call(
        kernel,
        out_shape=(
            jax.ShapeDtypeStruct((PIECE, NZ * WIDTH), BF16),
            jax.ShapeDtypeStruct((AROWS, WIDTH), BF16),
        ),
        in_specs=[hbm] * 6 + [vmem],
        out_specs=(vmem, vmem),
        scratch_shapes=[
            pltpu.VMEM((ROWS, WIDTH), BF16),
            pltpu.VMEM((ROWS, WIDTH), BF16),
            pltpu.VMEM((ROWS, WIDTH), BF16),
            pltpu.VMEM((4, WIDTH, 256), BF16),
            pltpu.VMEM((4, AUG, ROWS), BF16),
            pltpu.VMEM((NT, 2, AROWS, WIDTH), BF16),
            pltpu.VMEM((NT, AROWS, WIDTH), BF16),
            pltpu.VMEM((4, AUG, KEYS), BF16),
            pltpu.VMEM((4, WIDTH, 256), BF16),
            pltpu.VMEM((KEYS, 256), F32),
            pltpu.VMEM((KEYS, 256), F32),
            pltpu.VMEM((WIDTH, 256), F32),
            pltpu.VMEM((NZ, PIECE, WIDTH), BF16),
            pltpu.VMEM((NZ, PIECE, WIDTH), BF16),
            pltpu.VMEM((NT, AROWS, WIDTH), BF16),
            pltpu.VMEM((NT, AROWS, WIDTH), BF16),
            pltpu.VMEM((4, 2, 8, 128), F32),
            pltpu.VMEM((NT, 8, 128), F32),
            pltpu.VMEM((NT, 8, 128), F32),
            dma((6,)), dma((16,)), dma((16,)), dma((16,)), dma((16,)), dma((2,)), dma((2,)),
            dma((NZ,)), dma((NZ,)), dma((NT,)), dma((NT,)), dma((NT,)), dma((NT,)),
        ],
        compiler_params=pltpu.CompilerParams(
            collective_id=0, has_side_effects=True, vmem_limit_bytes=40 * 1024 * 1024),
    )(video_q, video_k, video_v, audio_q, audio_k, audio_v, norm_gain.reshape(1, -1))


def solution(mesh):
    placed = P("tok", "head")
    return jax.shard_map(
        shards,
        mesh=mesh,
        in_specs=(placed,) * 6 + (P(),),
        out_specs=(P(("tok", "head"), None), placed),
        check_vma=False,
    )
```

```python
import jax
import jax.numpy as jnp
from jax import lax
from jax.experimental import pallas as pl
from jax.experimental.pallas import tpu as pltpu
from jax.sharding import PartitionSpec as P

MESH = pl.DeviceIdType.MESH
F32, BF16 = jnp.float32, jnp.bfloat16
HEAD_DIM = 64
LOG2E = 1.4426950408889634
NZ = 8
NC = 16
ROWS = 896
PIECE = 112
AROWS = 32
WIDTH = 256
KEYS = 1024
BLOCK = 512

CHIPS = sorted(((dx, dy) for dx in range(4) for dy in range(4)),
               key=lambda d: -(min(d[0], 4 - d[0]) + min(d[1], 4 - d[1])))
CHIPS = CHIPS[-1:] + CHIPS[:-1]


def key_blocks(count):
    return [(start, min(BLOCK, count - start)) for start in range(0, count, BLOCK)]


def slot_of(d):
    return 2 * (d - 4) if d >= 4 else 2 * (3 - d) + 1


def loop(start, stop, body):
    def step(i, carry):
        body(i)
        return carry
    lax.fori_loop(start, stop, step, 0)


def kernel(vq, vk, vv, aq, ak, av, gain_hbm, vout, aout,
           gain, q_buf, k_buf, v_buf, qt, vt_local, kvg, qg, vt_audio, qt_audio,
           s_a, s_b, o_t, stage, recv, pass_o, pass_st, got_o, got_st,
           ret_stage, ret_recv, stat, stat_recv, w_buf,
           in_sem, kv_send, kv_recv, q_send, q_recv, fwd_send, fwd_recv, qf_send, qf_recv,
           z_send, z_recv, po_send, po_recv, ps_send, ps_recv,
           ret_send, ret_rsem, st_send, st_rsem):
    z = lax.axis_index("head")
    t = lax.axis_index("tok")
    x, y, c = t // 8, (t // 2) % 4, t % 2
    xs = [((x + i) % 4) * 8 + c for i in range(4)]
    ys = [((y + i) % 4) * 2 for i in range(4)]
    zs = [(z + i) % NZ for i in range(NZ)]
    sibling = (z, t + 1 - 2 * c)

    def chip(s, sign=1):
        dx, dy = CHIPS[s]
        return (z, xs[sign * dx % 4] + ys[sign * dy % 4])

    own = [
        pltpu.make_async_copy(src, dst, in_sem.at[i]) for i, (src, dst) in enumerate([
            (ak, kvg.at[0, 0]), (av, kvg.at[0, 1]), (aq, qg.at[0]),
            (vq, q_buf), (vv, v_buf), (vk, k_buf), (gain_hbm, gain)])
    ]
    for copy in own:
        copy.start()

    barrier = pltpu.get_barrier_semaphore()

    def greet(device):
        pl.semaphore_signal(barrier, inc=1, device_id=device, device_id_type=MESH)

    for d in (4, 3, 5, 2, 6, 1, 7):
        greet((zs[d], t))
    for s in range(1, NC):
        greet(chip(s))
    greet(sibling)
    for copy in own[:3]:
        copy.wait()
    pl.semaphore_wait(barrier, NZ - 1 + NC)

    def kv_copy(s):
        return pltpu.make_async_remote_copy(
            src_ref=kvg.at[0], dst_ref=kvg.at[s], send_sem=kv_send.at[s], recv_sem=kv_recv.at[s],
            device_id=chip(s, -1), device_id_type=MESH)

    def q_copy(s):
        return pltpu.make_async_remote_copy(
            src_ref=qg.at[0], dst_ref=qg.at[s], send_sem=q_send.at[s], recv_sem=q_recv.at[s],
            device_id=chip(s, -1), device_id_type=MESH)

    for s in range(1, NC):
        kv_copy(s).start()
    for s in range(1, NC):
        q_copy(s).start()

    own[3].wait()
    for j in range(4):
        parts = []
        for d in (4 + j, 3 - j):
            start = pl.multiple_of(zs[d] * PIECE, 16)
            parts.append(q_buf[pl.ds(start, PIECE), :])
            parts.append(jnp.zeros((128 - PIECE, WIDTH), BF16))
        qt[j] = jnp.concatenate(parts, axis=0).T * BF16(0.125)
    own[4].wait()
    for start in range(0, ROWS, 128):
        turned = v_buf[start:start + 128, :].T
        for h in range(4):
            vt_local[h, :, start:start + 128] = turned[h * HEAD_DIM:(h + 1) * HEAD_DIM]
    own[5].wait()
    own[6].wait()

    def kv_fwd(g):
        return pltpu.make_async_remote_copy(
            src_ref=kvg.at[4 * g:4 * g + 4], dst_ref=kvg.at[NC + 4 * g:NC + 4 * g + 4],
            send_sem=fwd_send.at[g], recv_sem=fwd_recv.at[g], device_id=sibling, device_id_type=MESH)

    def turn_values(g):
        turned = kvg[4 * g:4 * g + 4, 1].reshape(128, WIDTH).T
        for h in range(4):
            vt_audio[h, :, g * 128:g * 128 + 128] = turned[h * HEAD_DIM:(h + 1) * HEAD_DIM]

    for g in range(4):
        for s in range(max(4 * g, 1), 4 * g + 4):
            kv_copy(s).wait_recv()
        kv_fwd(g).start()
        turn_values(g)
    for g in range(4):
        kv_fwd(g).wait_recv()
        turn_values(4 + g)

    q_fwd = pltpu.make_async_remote_copy(
        src_ref=qg.at[0:NC], dst_ref=qg.at[NC:2 * NC], send_sem=qf_send, recv_sem=qf_recv,
        device_id=sibling, device_id_type=MESH)

    row = lax.broadcasted_iota(jnp.int32, (128, 256), 0)

    def masked(qt_ref, j, h):
        pair = qt_ref[j, (h // 2) * 128:(h // 2) * 128 + 128, :]
        keep = (row < HEAD_DIM) if h % 2 == 0 else (row >= HEAD_DIM)
        return jnp.where(keep, pair, jnp.zeros_like(pair))

    def audio_keys(start, size, h):
        lanes = slice((h // 2) * 128, (h // 2) * 128 + 128)
        return kvg[start // 32:(start + size) // 32, 0, :, lanes].reshape(size, 128)

    def video_keys(start, size, h):
        return k_buf[start:start + size, (h // 2) * 128:(h // 2) * 128 + 128]

    def both(first, second):
        top, acc, total = None, None, None
        if first is not None:
            keys, count, qt_ref, j, h, s_out = first
            q_head = masked(qt_ref, j, h)
        if second is not None:
            s_in, top_in, vt_ref, h_in, count = second
        for start, size in key_blocks(count):
            if first is not None:
                s = jnp.dot(keys(start, size, h), q_head, preferred_element_type=F32)
                s_out[start:start + size, :] = s
                part = jnp.max(s.reshape(size // 8, 8, 256), axis=0)
                top = part if top is None else jnp.maximum(top, part)
            if second is not None:
                w = jnp.exp2((s_in[start:start + size, :] - top_in) * LOG2E)
                part = jnp.sum(w.reshape(size // 8, 8, 256), axis=0)
                total = part if total is None else total + part
                o = jnp.dot(vt_ref[h_in, :, start:start + size], w.astype(BF16),
                            preferred_element_type=F32)
                acc = o if acc is None else acc + o
        if top is not None:
            top = jnp.max(top, axis=0, keepdims=True)
        if total is not None:
            total = jnp.sum(total, axis=0, keepdims=True)
        return top, acc, total

    def z_copy(d, slot):
        return pltpu.make_async_remote_copy(
            src_ref=stage.at[slot], dst_ref=recv.at[d], send_sem=z_send.at[d],
            recv_sem=z_recv.at[d], device_id=((z + d) % NZ, t), device_id_type=MESH)

    def video_chunk(j, top):
        after = jnp.minimum(j + 1, 3)
        steps = [(0, j, s_a), (1, j, s_b), (2, j, s_a), (3, j, s_b), (0, after, s_a)]
        for h in range(4):
            nh, nj, ns = steps[h + 1]
            top, acc, total = both((audio_keys, KEYS, qt, nj, nh, ns),
                                   (steps[h][2], top, vt_audio, h, KEYS))
            o_t[h * HEAD_DIM:(h + 1) * HEAD_DIM, :] = acc / total
        out = o_t[...].T.astype(BF16)
        stage[2 * j] = out[:PIECE]
        stage[2 * j + 1] = out[128:128 + PIECE]
        z_copy(4 + j, 2 * j).start()

        @pl.when(j < 3)
        def _():
            z_copy(3 - j, 2 * j + 1).start()

        @pl.when(j == 1)
        def _():
            for s in range(1, NC):
                q_copy(s).wait_recv()
            q_fwd.start()
        return top

    top, _, _ = both((audio_keys, KEYS, qt, 0, 0, s_a), None)
    lax.fori_loop(0, 4, video_chunk, top)

    q_fwd.wait_recv()
    for j in range(4):
        qt_audio[j] = qg[8 * j:8 * j + 8].reshape(256, WIDTH).T * BF16(0.125)

    def pass_copies(j):
        return (
            pltpu.make_async_remote_copy(
                src_ref=pass_o.at[j], dst_ref=got_o.at[j], send_sem=po_send.at[j],
                recv_sem=po_recv.at[j], device_id=sibling, device_id_type=MESH),
            pltpu.make_async_remote_copy(
                src_ref=pass_st.at[j], dst_ref=got_st.at[j], send_sem=ps_send.at[j],
                recv_sem=ps_recv.at[j], device_id=sibling, device_id_type=MESH))

    def ret_copies(s, device):
        return (
            pltpu.make_async_remote_copy(
                src_ref=ret_stage.at[s], dst_ref=ret_recv.at[s], send_sem=ret_send.at[s],
                recv_sem=ret_rsem.at[s], device_id=device, device_id_type=MESH),
            pltpu.make_async_remote_copy(
                src_ref=stat.at[s // 4], dst_ref=stat_recv.at[s], send_sem=st_send.at[s],
                recv_sem=st_rsem.at[s], device_id=device, device_id_type=MESH))

    def audio_heads(j, after, top, finish):
        steps = [(0, j, s_a), (1, j, s_b), (2, j, s_a), (3, j, s_b), (0, after, s_a)]
        for h in range(4):
            nh, nj, ns = steps[h + 1]
            top_h = top
            top, acc, total = both((video_keys, ROWS, qt_audio, nj, nh, ns),
                                   (steps[h][2], top_h, vt_local, h, ROWS))
            finish(h, top_h, acc, total)
        return top

    def pass_chunk(j, top):
        def finish(h, top_h, acc, total):
            pass_o[j, h * HEAD_DIM:(h + 1) * HEAD_DIM, :] = acc.astype(BF16)
            pass_st[j, h:h + 1, :] = top_h
            pass_st[j, 4 + h:5 + h, :] = total

        top = audio_heads(2 + j, (3 + j) % 4, top, finish)
        for copy in pass_copies(j):
            copy.start()
        return top

    top, _, _ = both((video_keys, ROWS, qt_audio, 2, 0, s_a), None)
    top = lax.fori_loop(0, 2, pass_chunk, top)

    for j in range(2):
        for copy in pass_copies(j):
            copy.wait_recv()

        def finish(h, top_h, acc, total, j=j):
            other_top = got_st[j, h:h + 1, :]
            peak = jnp.maximum(top_h, other_top)
            a = jnp.exp2((top_h - peak) * LOG2E)
            b = jnp.exp2((other_top - peak) * LOG2E)
            rows = slice(h * HEAD_DIM, (h + 1) * HEAD_DIM)
            o_t[rows, :] = acc * a + got_o[j, rows, :].astype(F32) * b
            norm = total * a + got_st[j, 4 + h:5 + h, :] * b
            for half in range(2):
                lanes = slice(half * 128, half * 128 + 128)
                stat[2 * j + half, h:h + 1, :] = peak[:, lanes]
                stat[2 * j + half, 4 + h:5 + h, :] = norm[:, lanes]

        top = audio_heads(j, min(j + 1, 1), top, finish)
        out = o_t[...].T.astype(BF16).reshape(8, AROWS, WIDTH)
        for p in range(8):
            s = 8 * j + p
            ret_stage[s] = out[p]
        for s in range(8 * j, 8 * j + 8):
            if s > 0:
                for copy in ret_copies(s, chip(s)):
                    copy.start()

    for d in range(1, NZ):
        z_copy(d, slot_of(d)).wait_recv()

    def received(d):
        return (stage[slot_of(0)] if d == 0 else recv[d]).astype(F32)

    total = None
    for d in range(NZ):
        wide = received(d)
        part = jnp.sum(wide * wide, axis=1, keepdims=True)
        total = part if total is None else total + part
    factor = lax.rsqrt(total * (1.0 / (NZ * WIDTH)) + 1e-06)
    for d in range(NZ):
        column = pl.multiple_of(((z + NZ - d) % NZ) * WIDTH, WIDTH)
        lanes = pl.ds(column, WIDTH)
        vout[:, lanes] = (received(d) * factor * gain[:, lanes]).astype(BF16)

    for s in range(1, NC):
        for copy in ret_copies(s, chip(s)):
            copy.wait_recv()
    tiles = []
    for s in range(NC):
        tile = stat[0] if s == 0 else stat_recv[s]
        shift = (128 - 32 * (s % 4)) % 128
        tiles.append(pltpu.roll(tile, shift, 1) if shift else tile)
    peak = tiles[0]
    for tile in tiles[1:]:
        peak = jnp.maximum(peak, tile)
    norm = None
    weights = []
    for tile in tiles:
        w = jnp.exp2((tile - peak) * LOG2E)
        weights.append(w)
        part = w * pltpu.roll(tile, 4, 0)
        norm = part if norm is None else norm + part
    for s in range(NC):
        w_buf[s] = weights[s] / norm
    turned = w_buf[...].reshape(NC * 8, 128).T[:AROWS]
    lane = lax.broadcasted_iota(jnp.int32, (AROWS, 128), 1)
    for pair in range(2):
        lanes = slice(pair * 128, pair * 128 + 128)
        merged = None
        for s in range(NC):
            at = s * 8 + 2 * pair
            w = jnp.where(lane < HEAD_DIM, turned[:, at:at + 1], turned[:, at + 1:at + 2])
            part = w * (ret_stage[0, :, lanes] if s == 0 else ret_recv[s, :, lanes]).astype(F32)
            merged = part if merged is None else merged + part
        aout[:, lanes] = merged.astype(BF16)

    for s in range(1, NC):
        kv_copy(s).wait_send()
        q_copy(s).wait_send()
    for g in range(4):
        kv_fwd(g).wait_send()
    q_fwd.wait_send()
    for d in range(1, NZ):
        z_copy(d, slot_of(d)).wait_send()
    for j in range(2):
        for copy in pass_copies(j):
            copy.wait_send()
    for s in range(1, NC):
        for copy in ret_copies(s, chip(s)):
            copy.wait_send()


def shards(video_q, video_k, video_v, audio_q, audio_k, audio_v, norm_gain):
    arrays = (video_q, video_k, video_v, audio_q, audio_k, audio_v, norm_gain.reshape(1, -1))
    arrays = [pltpu.with_memory_space_constraint(a, pltpu.HBM) for a in arrays]
    vmem = pl.BlockSpec(memory_space=pltpu.VMEM)
    dma = pltpu.SemaphoreType.DMA
    return pl.pallas_call(
        kernel,
        out_shape=(
            jax.ShapeDtypeStruct((PIECE, NZ * WIDTH), BF16),
            jax.ShapeDtypeStruct((AROWS, WIDTH), BF16),
        ),
        in_specs=[pl.BlockSpec(memory_space=pltpu.HBM)] * 7,
        out_specs=(vmem, vmem),
        scratch_shapes=[
            pltpu.VMEM((1, NZ * WIDTH), F32),
            pltpu.VMEM((ROWS, WIDTH), BF16),
            pltpu.VMEM((ROWS, WIDTH), BF16),
            pltpu.VMEM((ROWS, WIDTH), BF16),
            pltpu.VMEM((4, WIDTH, 256), BF16),
            pltpu.VMEM((4, HEAD_DIM, ROWS), BF16),
            pltpu.VMEM((2 * NC, 2, AROWS, WIDTH), BF16),
            pltpu.VMEM((2 * NC, AROWS, WIDTH), BF16),
            pltpu.VMEM((4, HEAD_DIM, KEYS), BF16),
            pltpu.VMEM((4, WIDTH, 256), BF16),
            pltpu.VMEM((KEYS, 256), F32),
            pltpu.VMEM((KEYS, 256), F32),
            pltpu.VMEM((WIDTH, 256), F32),
            pltpu.VMEM((NZ, PIECE, WIDTH), BF16),
            pltpu.VMEM((NZ, PIECE, WIDTH), BF16),
            pltpu.VMEM((2, WIDTH, 256), BF16),
            pltpu.VMEM((2, 8, 256), F32),
            pltpu.VMEM((2, WIDTH, 256), BF16),
            pltpu.VMEM((2, 8, 256), F32),
            pltpu.VMEM((NC, AROWS, WIDTH), BF16),
            pltpu.VMEM((NC, AROWS, WIDTH), BF16),
            pltpu.VMEM((4, 8, 128), F32),
            pltpu.VMEM((NC, 8, 128), F32),
            pltpu.VMEM((NC, 8, 128), F32),
            dma((7,)), dma((NC,)), dma((NC,)), dma((NC,)), dma((NC,)), dma((4,)), dma((4,)),
            dma, dma, dma((NZ,)), dma((NZ,)), dma((2,)), dma((2,)), dma((2,)), dma((2,)),
            dma((NC,)), dma((NC,)), dma((NC,)), dma((NC,)),
        ],
        compiler_params=pltpu.CompilerParams(
            collective_id=0, has_side_effects=True, vmem_limit_bytes=24 * 1024 * 1024),
    )(*arrays)


def solution(mesh):
    placed = P("tok", "head")
    return jax.shard_map(
        shards,
        mesh=mesh,
        in_specs=(placed,) * 6 + (P(),),
        out_specs=(P(("tok", "head"), None), placed),
        check_vma=False,
    )
```

```python
import jax
import jax.numpy as jnp
from jax import lax
from jax.experimental import pallas as pl
from jax.experimental.pallas import tpu as pltpu
from jax.sharding import PartitionSpec as P

MESH = pl.DeviceIdType.MESH
F32, BF16 = jnp.float32, jnp.bfloat16
HEAD_DIM = 64
LOG2E = 1.4426950408889634
NZ = 8
NC = 16
ROWS = 896
PIECE = 112
AROWS = 32
WIDTH = 256
KEYS = 1024
BLOCK = 512
BEFORE = 3

CHIPS = sorted(((dx, dy) for dx in range(4) for dy in range(4)),
               key=lambda d: -(min(d[0], 4 - d[0]) + min(d[1], 4 - d[1])))
CHIPS = CHIPS[-1:] + CHIPS[:-1]


def key_blocks(count):
    return [(start, min(BLOCK, count - start)) for start in range(0, count, BLOCK)]


def slot_of(d):
    if d == 0:
        return 1
    return 2 * (4 - d) if d <= 4 else 2 * (d - 4) + 1


def loop(start, stop, body):
    def step(i, carry):
        body(i)
        return carry
    lax.fori_loop(start, stop, step, 0)


def kernel(vq, vk, vv, aq, ak, av, gain_hbm, vout, ret_recv, stat_recv,
           gain, q_buf, k_buf, v_buf, qt, vt_local, kvg, qg, vt_audio, qt_audio,
           s_a, s_b, s_c, s_d, o_t, stage, recv, pass_o, pass_st, got_o, got_st,
           ret_stage, stat,
           in_sem, kv_send, kv_recv, q_send, q_recv, fwd_send, fwd_recv, qf_send, qf_recv,
           z_send, z_recv, po_send, po_recv, ps_send, ps_recv,
           ret_send, ret_rsem, st_send, st_rsem):
    z = lax.axis_index("head")
    t = lax.axis_index("tok")
    x, y, c = t // 8, (t // 2) % 4, t % 2
    xs = [((x + i) % 4) * 8 + c for i in range(4)]
    ys = [((y + i) % 4) * 2 for i in range(4)]
    zs = [(z + i) % NZ for i in range(NZ)]
    sibling = (z, t + 1 - 2 * c)

    def chip(s, sign=1):
        dx, dy = CHIPS[s]
        return (z, xs[sign * dx % 4] + ys[sign * dy % 4])

    barrier = pltpu.get_barrier_semaphore()
    peers = [(min(d, NZ - d), (zs[d], t)) for d in range(1, NZ)]
    peers += [(min(CHIPS[i][0], 4 - CHIPS[i][0]) + min(CHIPS[i][1], 4 - CHIPS[i][1]), chip(i))
              for i in range(1, NC)]
    for _, device in sorted(peers, key=lambda peer: -peer[0]) + [(0, sibling)]:
        pl.semaphore_signal(barrier, inc=1, device_id=device, device_id_type=MESH)

    own = [
        pltpu.make_async_copy(src, dst, in_sem.at[i]) for i, (src, dst) in enumerate([
            (ak.at[:, 0:128], kvg.at[0, 0, 0]), (av.at[:, 0:128], kvg.at[0, 0, 1]),
            (ak.at[:, 128:256], kvg.at[1, 0, 0]), (av.at[:, 128:256], kvg.at[1, 0, 1]),
            (aq, qg.at[0]), (vq, q_buf), (vv, v_buf), (vk, k_buf), (gain_hbm, gain)])
    ]
    for copy in own:
        copy.start()

    for copy in own[:5]:
        copy.wait()
    pl.semaphore_wait(barrier, NZ - 1 + NC)

    def kv_copy(pair, s):
        return pltpu.make_async_remote_copy(
            src_ref=kvg.at[pair, 0], dst_ref=kvg.at[pair, s], send_sem=kv_send.at[pair, s],
            recv_sem=kv_recv.at[pair, s], device_id=chip(s, -1), device_id_type=MESH)

    def q_copy(s):
        return pltpu.make_async_remote_copy(
            src_ref=qg.at[0], dst_ref=qg.at[s], send_sem=q_send.at[s], recv_sem=q_recv.at[s],
            device_id=chip(s, -1), device_id_type=MESH)

    for pair in range(2):
        for s in range(1, NC):
            kv_copy(pair, s).start()
    for s in range(1, NC):
        q_copy(s).start()

    own[5].wait()
    for j in range(4):
        parts = []
        for d in (4 - j, 4 + j if j else 0):
            start = pl.multiple_of(zs[d] * PIECE, 16)
            parts.append(q_buf[pl.ds(start, PIECE), :])
            parts.append(jnp.zeros((128 - PIECE, WIDTH), BF16))
        qt[j] = jnp.concatenate(parts, axis=0).T * BF16(0.125)
    own[6].wait()
    for start in range(0, ROWS, 128):
        turned = v_buf[start:start + 128, :].T
        for h in range(4):
            vt_local[h, :, start:start + 128] = turned[h * HEAD_DIM:(h + 1) * HEAD_DIM]
    own[7].wait()
    own[8].wait()

    def kv_fwd(pair, g):
        return pltpu.make_async_remote_copy(
            src_ref=kvg.at[pair, 4 * g:4 * g + 4], dst_ref=kvg.at[pair, NC + 4 * g:NC + 4 * g + 4],
            send_sem=fwd_send.at[pair, g], recv_sem=fwd_recv.at[pair, g], device_id=sibling,
            device_id_type=MESH)

    def turn_values(pair, g):
        turned = kvg[pair, 4 * g:4 * g + 4, 1].reshape(128, 128).T
        for h in range(2):
            vt_audio[2 * pair + h, :, g * 128:g * 128 + 128] = turned[h * HEAD_DIM:(h + 1) * HEAD_DIM]

    def pass_on(pair):
        for g in range(4):
            for s in range(max(4 * g, 1), 4 * g + 4):
                kv_copy(pair, s).wait_recv()
            kv_fwd(pair, g).start()

    pass_on(0)
    for g in range(4):
        turn_values(0, g)
    for g in range(4):
        kv_fwd(0, g).wait_recv()
        turn_values(0, 4 + g)

    q_fwd = pltpu.make_async_remote_copy(
        src_ref=qg.at[0:NC], dst_ref=qg.at[NC:2 * NC], send_sem=qf_send, recv_sem=qf_recv,
        device_id=sibling, device_id_type=MESH)

    row = lax.broadcasted_iota(jnp.int32, (128, 256), 0)

    def masked(qt_ref, j, h):
        pair = qt_ref[j, (h // 2) * 128:(h // 2) * 128 + 128, :]
        keep = (row < HEAD_DIM) if h % 2 == 0 else (row >= HEAD_DIM)
        return jnp.where(keep, pair, jnp.zeros_like(pair))

    def audio_keys(start, size, h):
        return kvg[h // 2, start // 32:(start + size) // 32, 0].reshape(size, 128)

    def video_keys(start, size, h):
        return k_buf[start:start + size, (h // 2) * 128:(h // 2) * 128 + 128]

    def both(first, second):
        top, acc, total = None, None, None
        if first is not None:
            keys, count, qt_ref, j, h, s_out = first
            q_head = masked(qt_ref, j, h)
        if second is not None:
            s_in, top_in, vt_ref, h_in, count = second
        for start, size in key_blocks(count):
            if first is not None:
                s = jnp.dot(keys(start, size, h), q_head, preferred_element_type=F32)
                s_out[start:start + size, :] = s
                part = jnp.max(s.reshape(size // 8, 8, 256), axis=0)
                top = part if top is None else jnp.maximum(top, part)
            if second is not None:
                w = jnp.exp2((s_in[start:start + size, :] - top_in) * LOG2E)
                part = jnp.sum(w.reshape(size // 8, 8, 256), axis=0)
                total = part if total is None else total + part
                o = jnp.dot(vt_ref[h_in, :, start:start + size], w.astype(BF16),
                            preferred_element_type=F32)
                acc = o if acc is None else acc + o
        if top is not None:
            top = jnp.max(top, axis=0, keepdims=True)
        if total is not None:
            total = jnp.sum(total, axis=0, keepdims=True)
        return top, acc, total

    def z_copy(pair, d, slot):
        return pltpu.make_async_remote_copy(
            src_ref=stage.at[pair, slot], dst_ref=recv.at[pair, d], send_sem=z_send.at[pair, d],
            recv_sem=z_recv.at[pair, d], device_id=((z + d) % NZ, t), device_id_type=MESH)

    def video_chunk(pair, at_one, j, top):
        after = jnp.minimum(j + 1, 3)
        h0, h1 = 2 * pair, 2 * pair + 1
        top, acc, total = both((audio_keys, KEYS, qt, j, h1, s_b), (s_a, top, vt_audio, h0, KEYS))
        o_t[:HEAD_DIM, :] = acc / total
        top, acc, total = both((audio_keys, KEYS, qt, after, h0, s_a), (s_b, top, vt_audio, h1, KEYS))
        o_t[HEAD_DIM:2 * HEAD_DIM, :] = acc / total
        out = o_t[:2 * HEAD_DIM, :].T.astype(BF16)
        stage[pair, 2 * j] = out[:PIECE]
        stage[pair, 2 * j + 1] = out[128:128 + PIECE]
        z_copy(pair, 4 - j, 2 * j).start()

        @pl.when(j > 0)
        def _():
            z_copy(pair, 4 + j, 2 * j + 1).start()

        pl.when(j == 1 - pair)(at_one)
        return top

    def video_start(pair):
        return both((audio_keys, KEYS, qt, 0, 2 * pair, s_a), None)[0]

    def video_chunks(pair, start, stop, at_one, top):
        return lax.fori_loop(start, stop, lambda j, top: video_chunk(pair, at_one, j, top), top)

    def pass_queries():
        for s in range(1, NC):
            q_copy(s).wait_recv()
        q_fwd.start()

    video_chunks(0, 0, 4, lambda: pass_on(1), video_start(0))
    for g in range(4):
        turn_values(1, g)
    for g in range(4):
        kv_fwd(1, g).wait_recv()
        turn_values(1, 4 + g)
    video_top = video_chunks(1, 0, BEFORE, pass_queries, video_start(1))

    q_fwd.wait_recv()
    for j in range(4):
        qt_audio[j] = qg[8 * j:8 * j + 8].reshape(256, WIDTH).T * BF16(0.125)

    def pass_copies(j):
        return (
            pltpu.make_async_remote_copy(
                src_ref=pass_o.at[j], dst_ref=got_o.at[j], send_sem=po_send.at[j],
                recv_sem=po_recv.at[j], device_id=sibling, device_id_type=MESH),
            pltpu.make_async_remote_copy(
                src_ref=pass_st.at[j], dst_ref=got_st.at[j], send_sem=ps_send.at[j],
                recv_sem=ps_recv.at[j], device_id=sibling, device_id_type=MESH))

    def ret_copies(s, device):
        return (
            pltpu.make_async_remote_copy(
                src_ref=ret_stage.at[s], dst_ref=ret_recv.at[s], send_sem=ret_send.at[s],
                recv_sem=ret_rsem.at[s], device_id=device, device_id_type=MESH),
            pltpu.make_async_remote_copy(
                src_ref=stat.at[s // 4], dst_ref=stat_recv.at[s], send_sem=st_send.at[s],
                recv_sem=st_rsem.at[s], device_id=device, device_id_type=MESH))

    def audio_heads(j, after, top, finish):
        steps = [(0, j, s_c), (1, j, s_d), (2, j, s_c), (3, j, s_d), (0, after, s_c)]
        for h in range(4):
            nh, nj, ns = steps[h + 1]
            top_h = top
            top, acc, total = both((video_keys, ROWS, qt_audio, nj, nh, ns),
                                   (steps[h][2], top_h, vt_local, h, ROWS))
            finish(h, top_h, acc, total)
        return top

    def pass_chunk(j, top):
        def finish(h, top_h, acc, total):
            pass_o[j, h * HEAD_DIM:(h + 1) * HEAD_DIM, :] = acc.astype(BF16)
            pass_st[j, h:h + 1, :] = top_h
            pass_st[j, 4 + h:5 + h, :] = total

        top = audio_heads(2 + j, (3 + j) % 4, top, finish)
        for copy in pass_copies(j):
            copy.start()
        return top

    top, _, _ = both((video_keys, ROWS, qt_audio, 2, 0, s_c), None)
    top = lax.fori_loop(0, 2, pass_chunk, top)

    for j in range(2):
        for copy in pass_copies(j):
            copy.wait_recv()

        def finish(h, top_h, acc, total, j=j):
            other_top = got_st[j, h:h + 1, :]
            peak = jnp.maximum(top_h, other_top)
            a = jnp.exp2((top_h - peak) * LOG2E)
            b = jnp.exp2((other_top - peak) * LOG2E)
            rows = slice(h * HEAD_DIM, (h + 1) * HEAD_DIM)
            o_t[rows, :] = acc * a + got_o[j, rows, :].astype(F32) * b
            norm = total * a + got_st[j, 4 + h:5 + h, :] * b
            for half in range(2):
                lanes = slice(half * 128, half * 128 + 128)
                stat[2 * j + half, h:h + 1, :] = peak[:, lanes]
                stat[2 * j + half, 4 + h:5 + h, :] = norm[:, lanes]

        top = audio_heads(j, min(j + 1, 1), top, finish)
        out = o_t[...].T.astype(BF16).reshape(8, AROWS, WIDTH)
        for p in range(8):
            s = 8 * j + p
            ret_stage[s] = out[p]
        for s in range(8 * j, 8 * j + 8):
            if s > 0:
                for copy in ret_copies(s, chip(s)):
                    copy.start()
    if BEFORE < 4:
        video_chunks(1, BEFORE, 4, pass_queries, video_top)
    ret_recv[0] = ret_stage[0]
    stat_recv[0] = stat[0]

    for pair in range(2):
        for d in range(1, NZ):
            z_copy(pair, d, slot_of(d)).wait_recv()

    def received(pair, d):
        return (stage[pair, slot_of(0)] if d == 0 else recv[pair, d]).astype(F32)

    total = None
    for pair in range(2):
        for d in range(NZ):
            wide = received(pair, d)
            part = jnp.sum(wide * wide, axis=1, keepdims=True)
            total = part if total is None else total + part
    factor = lax.rsqrt(total * (1.0 / (NZ * WIDTH)) + 1e-06)
    for d in range(NZ):
        for pair in range(2):
            column = pl.multiple_of(((z + NZ - d) % NZ) * WIDTH + 128 * pair, 128)
            lanes = pl.ds(column, 128)
            vout[:, lanes] = (received(pair, d) * factor * gain[:, lanes]).astype(BF16)

    for s in range(1, NC):
        for copy in ret_copies(s, chip(s)):
            copy.wait_recv()

    for s in range(1, NC):
        kv_copy(0, s).wait_send()
        kv_copy(1, s).wait_send()
        q_copy(s).wait_send()
    for g in range(4):
        kv_fwd(0, g).wait_send()
        kv_fwd(1, g).wait_send()
    q_fwd.wait_send()
    for d in range(1, NZ):
        z_copy(0, d, slot_of(d)).wait_send()
        z_copy(1, d, slot_of(d)).wait_send()
    for j in range(2):
        for copy in pass_copies(j):
            copy.wait_send()
    for s in range(1, NC):
        for copy in ret_copies(s, chip(s)):
            copy.wait_send()


def finish_kernel(rows, ret_recv, stat_recv, vout, aout, merged_buf, w_buf, sem):
    rows_out = pltpu.make_async_copy(rows, vout, sem.at[0])
    rows_out.start()
    tiles = []
    for s in range(NC):
        tile = stat_recv[s]
        shift = (128 - 32 * (s % 4)) % 128
        tiles.append(pltpu.roll(tile, shift, 1) if shift else tile)
    peak = tiles[0]
    for tile in tiles[1:]:
        peak = jnp.maximum(peak, tile)
    norm = None
    weights = []
    for tile in tiles:
        w = jnp.exp2((tile - peak) * LOG2E)
        weights.append(w)
        part = w * pltpu.roll(tile, 4, 0)
        norm = part if norm is None else norm + part
    for s in range(NC):
        w_buf[s] = weights[s] / norm
    turned = w_buf[...].reshape(NC * 8, 128).T[:AROWS]
    lane = lax.broadcasted_iota(jnp.int32, (AROWS, 128), 1)
    for pair in range(2):
        lanes = slice(pair * 128, pair * 128 + 128)
        merged = None
        for s in range(NC):
            at = s * 8 + 2 * pair
            w = jnp.where(lane < HEAD_DIM, turned[:, at:at + 1], turned[:, at + 1:at + 2])
            part = w * ret_recv[s, :, lanes].astype(F32)
            merged = part if merged is None else merged + part
        merged_buf[:, lanes] = merged.astype(BF16)
    merged_out = pltpu.make_async_copy(merged_buf, aout, sem.at[1])
    merged_out.start()
    merged_out.wait()
    rows_out.wait()


def shards(video_q, video_k, video_v, audio_q, audio_k, audio_v, norm_gain):
    arrays = (video_q, video_k, video_v, audio_q, audio_k, audio_v, norm_gain.reshape(1, -1))
    arrays = [pltpu.with_memory_space_constraint(a, pltpu.HBM) for a in arrays]
    vmem = pl.BlockSpec(memory_space=pltpu.VMEM)
    dma = pltpu.SemaphoreType.DMA
    rows, ret_recv, stat_recv = pl.pallas_call(
        kernel,
        out_shape=(
            jax.ShapeDtypeStruct((PIECE, NZ * WIDTH), BF16),
            jax.ShapeDtypeStruct((NC, AROWS, WIDTH), BF16),
            jax.ShapeDtypeStruct((NC, 8, 128), F32),
        ),
        in_specs=[pl.BlockSpec(memory_space=pltpu.HBM)] * 7,
        out_specs=(vmem, vmem, vmem),
        scratch_shapes=[
            pltpu.VMEM((1, NZ * WIDTH), F32),
            pltpu.VMEM((ROWS, WIDTH), BF16),
            pltpu.VMEM((ROWS, WIDTH), BF16),
            pltpu.VMEM((ROWS, WIDTH), BF16),
            pltpu.VMEM((4, WIDTH, 256), BF16),
            pltpu.VMEM((4, HEAD_DIM, ROWS), BF16),
            pltpu.VMEM((2, 2 * NC, 2, AROWS, 128), BF16),
            pltpu.VMEM((2 * NC, AROWS, WIDTH), BF16),
            pltpu.VMEM((4, HEAD_DIM, KEYS), BF16),
            pltpu.VMEM((4, WIDTH, 256), BF16),
            pltpu.VMEM((KEYS, 256), F32),
            pltpu.VMEM((KEYS, 256), F32),
            pltpu.VMEM((ROWS, 256), F32),
            pltpu.VMEM((ROWS, 256), F32),
            pltpu.VMEM((WIDTH, 256), F32),
            pltpu.VMEM((2, NZ, PIECE, 128), BF16),
            pltpu.VMEM((2, NZ, PIECE, 128), BF16),
            pltpu.VMEM((2, WIDTH, 256), BF16),
            pltpu.VMEM((2, 8, 256), F32),
            pltpu.VMEM((2, WIDTH, 256), BF16),
            pltpu.VMEM((2, 8, 256), F32),
            pltpu.VMEM((NC, AROWS, WIDTH), BF16),
            pltpu.VMEM((4, 8, 128), F32),
            dma((9,)), dma((2, NC)), dma((2, NC)), dma((NC,)), dma((NC,)), dma((2, 4)), dma((2, 4)),
            dma, dma, dma((2, NZ)), dma((2, NZ)), dma((2,)), dma((2,)), dma((2,)), dma((2,)),
            dma((NC,)), dma((NC,)), dma((NC,)), dma((NC,)),
        ],
        compiler_params=pltpu.CompilerParams(
            collective_id=0, has_side_effects=True, vmem_limit_bytes=24 * 1024 * 1024),
    )(*arrays)
    return pl.pallas_call(
        finish_kernel,
        out_shape=(
            jax.ShapeDtypeStruct((PIECE, NZ * WIDTH), BF16),
            jax.ShapeDtypeStruct((AROWS, WIDTH), BF16),
        ),
        in_specs=[vmem] * 3,
        out_specs=(pl.BlockSpec(memory_space=pltpu.HBM),) * 2,
        scratch_shapes=[
            pltpu.VMEM((AROWS, WIDTH), BF16),
            pltpu.VMEM((NC, 8, 128), F32),
            dma((2,)),
        ],
        compiler_params=pltpu.CompilerParams(vmem_limit_bytes=4 * 1024 * 1024),
    )(rows, ret_recv, stat_recv)


def solution(mesh):
    placed = P("tok", "head")
    return jax.shard_map(
        shards,
        mesh=mesh,
        in_specs=(placed,) * 6 + (P(),),
        out_specs=(P(("tok", "head"), None), placed),
        check_vma=False,
    )
```

```python
import jax
import jax.numpy as jnp
from jax import lax
from jax.experimental import pallas as pl
from jax.experimental.pallas import tpu as pltpu
from jax.sharding import PartitionSpec as P

MESH = pl.DeviceIdType.MESH
F32, BF16 = jnp.float32, jnp.bfloat16
HEAD_DIM = 64
LOG2E = 1.4426950408889634
NZ = 8
NC = 16
ROWS = 896
PIECE = 112
AROWS = 32
WIDTH = 256
KEYS = 1024
BLOCK = 512
BEFORE = 2

CHIPS = sorted(((dx, dy) for dx in range(4) for dy in range(4)),
               key=lambda d: -(min(d[0], 4 - d[0]) + min(d[1], 4 - d[1])))
CHIPS = CHIPS[-1:] + CHIPS[:-1]


def key_blocks(count):
    return [(start, min(BLOCK, count - start)) for start in range(0, count, BLOCK)]


def slot_of(d):
    if d == 0:
        return 1
    return 2 * (4 - d) if d <= 4 else 2 * (d - 4) + 1


def loop(start, stop, body):
    def step(i, carry):
        body(i)
        return carry
    lax.fori_loop(start, stop, step, 0)


def kernel(vq, vk, vv, aq, ak, av, gain_hbm, vout, ret_recv, stat_recv,
           gain, q_buf, k_buf, v_buf, qt, vt_local, kvg, qg, vt_audio, qt_audio,
           s_a, s_b, s_c, s_d, o_t, stage, recv, pass_o, pass_st, got_o, got_st,
           ret_stage, stat,
           in_sem, kv_send, kv_recv, q_send, q_recv, fwd_send, fwd_recv, qf_send, qf_recv,
           z_send, z_recv, po_send, po_recv, ps_send, ps_recv,
           ret_send, ret_rsem, st_send, st_rsem):
    z = lax.axis_index("head")
    t = lax.axis_index("tok")
    x, y, c = t // 8, (t // 2) % 4, t % 2
    xs = [((x + i) % 4) * 8 + c for i in range(4)]
    ys = [((y + i) % 4) * 2 for i in range(4)]
    zs = [(z + i) % NZ for i in range(NZ)]
    sibling = (z, t + 1 - 2 * c)

    def chip(s, sign=1):
        dx, dy = CHIPS[s]
        return (z, xs[sign * dx % 4] + ys[sign * dy % 4])

    barrier = pltpu.get_barrier_semaphore()
    peers = [(min(d, NZ - d), (zs[d], t)) for d in range(1, NZ)]
    peers += [(min(CHIPS[i][0], 4 - CHIPS[i][0]) + min(CHIPS[i][1], 4 - CHIPS[i][1]), chip(i))
              for i in range(1, NC)]
    for _, device in sorted(peers, key=lambda peer: -peer[0]) + [(0, sibling)]:
        pl.semaphore_signal(barrier, inc=1, device_id=device, device_id_type=MESH)

    own = [
        pltpu.make_async_copy(src, dst, in_sem.at[i]) for i, (src, dst) in enumerate([
            (ak.at[:, 0:128], kvg.at[0, 0, 0]), (av.at[:, 0:128], kvg.at[0, 0, 1]),
            (ak.at[:, 128:256], kvg.at[1, 0, 0]), (av.at[:, 128:256], kvg.at[1, 0, 1]),
            (aq, qg.at[0]), (vq, q_buf), (vv, v_buf), (vk, k_buf), (gain_hbm, gain)])
    ]
    for copy in own:
        copy.start()

    for copy in own[:5]:
        copy.wait()
    pl.semaphore_wait(barrier, NZ - 1 + NC)

    def kv_copy(pair, s):
        return pltpu.make_async_remote_copy(
            src_ref=kvg.at[pair, 0], dst_ref=kvg.at[pair, s], send_sem=kv_send.at[pair, s],
            recv_sem=kv_recv.at[pair, s], device_id=chip(s, -1), device_id_type=MESH)

    def q_copy(s):
        return pltpu.make_async_remote_copy(
            src_ref=qg.at[0], dst_ref=qg.at[s], send_sem=q_send.at[s], recv_sem=q_recv.at[s],
            device_id=chip(s, -1), device_id_type=MESH)

    for s in range(1, NC):
        kv_copy(0, s).start()
    for s in range(1, NC):
        q_copy(s).start()
    for s in range(1, NC):
        kv_copy(1, s).start()

    own[5].wait()
    for j in range(4):
        parts = []
        for d in (4 - j, 4 + j if j else 0):
            start = pl.multiple_of(zs[d] * PIECE, 16)
            parts.append(q_buf[pl.ds(start, PIECE), :])
            parts.append(jnp.zeros((128 - PIECE, WIDTH), BF16))
        qt[j] = jnp.concatenate(parts, axis=0).T * BF16(0.125)
    own[6].wait()
    for start in range(0, ROWS, 128):
        turned = v_buf[start:start + 128, :].T
        for h in range(4):
            vt_local[h, :, start:start + 128] = turned[h * HEAD_DIM:(h + 1) * HEAD_DIM]
    own[7].wait()
    own[8].wait()

    def kv_fwd(pair, g):
        return pltpu.make_async_remote_copy(
            src_ref=kvg.at[pair, 4 * g:4 * g + 4], dst_ref=kvg.at[pair, NC + 4 * g:NC + 4 * g + 4],
            send_sem=fwd_send.at[pair, g], recv_sem=fwd_recv.at[pair, g], device_id=sibling,
            device_id_type=MESH)

    def turn_values(pair, g):
        turned = kvg[pair, 4 * g:4 * g + 4, 1].reshape(128, 128).T
        for h in range(2):
            vt_audio[2 * pair + h, :, g * 128:g * 128 + 128] = turned[h * HEAD_DIM:(h + 1) * HEAD_DIM]

    def pass_on(pair):
        for g in range(4):
            for s in range(max(4 * g, 1), 4 * g + 4):
                kv_copy(pair, s).wait_recv()
            kv_fwd(pair, g).start()

    pass_on(0)
    for g in range(4):
        turn_values(0, g)
    for g in range(4):
        kv_fwd(0, g).wait_recv()
        turn_values(0, 4 + g)

    q_fwd = pltpu.make_async_remote_copy(
        src_ref=qg.at[0:NC], dst_ref=qg.at[NC:2 * NC], send_sem=qf_send, recv_sem=qf_recv,
        device_id=sibling, device_id_type=MESH)

    row = lax.broadcasted_iota(jnp.int32, (128, 256), 0)

    def masked(qt_ref, j, h):
        pair = qt_ref[j, (h // 2) * 128:(h // 2) * 128 + 128, :]
        keep = (row < HEAD_DIM) if h % 2 == 0 else (row >= HEAD_DIM)
        return jnp.where(keep, pair, jnp.zeros_like(pair))

    def audio_keys(start, size, h):
        return kvg[h // 2, start // 32:(start + size) // 32, 0].reshape(size, 128)

    def video_keys(start, size, h):
        return k_buf[start:start + size, (h // 2) * 128:(h // 2) * 128 + 128]

    def both(first, second):
        top, acc, total = None, None, None
        if first is not None:
            keys, count, qt_ref, j, h, s_out = first
            q_head = masked(qt_ref, j, h)
        if second is not None:
            s_in, top_in, vt_ref, h_in, count = second
        for start, size in key_blocks(count):
            if first is not None:
                s = jnp.dot(keys(start, size, h), q_head, preferred_element_type=F32)
                s_out[start:start + size, :] = s
                part = jnp.max(s.reshape(size // 8, 8, 256), axis=0)
                top = part if top is None else jnp.maximum(top, part)
            if second is not None:
                w = jnp.exp2((s_in[start:start + size, :] - top_in) * LOG2E)
                part = jnp.sum(w.reshape(size // 8, 8, 256), axis=0)
                total = part if total is None else total + part
                o = jnp.dot(vt_ref[h_in, :, start:start + size], w.astype(BF16),
                            preferred_element_type=F32)
                acc = o if acc is None else acc + o
        if top is not None:
            top = jnp.max(top, axis=0, keepdims=True)
        if total is not None:
            total = jnp.sum(total, axis=0, keepdims=True)
        return top, acc, total

    def z_copy(pair, d, slot):
        return pltpu.make_async_remote_copy(
            src_ref=stage.at[pair, slot], dst_ref=recv.at[pair, d], send_sem=z_send.at[pair, d],
            recv_sem=z_recv.at[pair, d], device_id=((z + d) % NZ, t), device_id_type=MESH)

    def video_chunk(pair, at_one, j, top):
        after = jnp.minimum(j + 1, 3)
        h0, h1 = 2 * pair, 2 * pair + 1
        top, acc, total = both((audio_keys, KEYS, qt, j, h1, s_b), (s_a, top, vt_audio, h0, KEYS))
        o_t[:HEAD_DIM, :] = acc / total
        top, acc, total = both((audio_keys, KEYS, qt, after, h0, s_a), (s_b, top, vt_audio, h1, KEYS))
        o_t[HEAD_DIM:2 * HEAD_DIM, :] = acc / total
        out = o_t[:2 * HEAD_DIM, :].T.astype(BF16)
        stage[pair, 2 * j] = out[:PIECE]
        stage[pair, 2 * j + 1] = out[128:128 + PIECE]
        z_copy(pair, 4 - j, 2 * j).start()

        @pl.when(j > 0)
        def _():
            z_copy(pair, 4 + j, 2 * j + 1).start()

        if at_one is not None:
            pl.when(j == 1)(at_one)
        return top

    def video_start(pair):
        return both((audio_keys, KEYS, qt, 0, 2 * pair, s_a), None)[0]

    def video_chunks(pair, start, stop, at_one, top):
        return lax.fori_loop(start, stop, lambda j, top: video_chunk(pair, at_one, j, top), top)

    def pass_queries():
        for s in range(1, NC):
            q_copy(s).wait_recv()
        q_fwd.start()

    video_chunks(0, 0, 4, pass_queries, video_start(0))

    q_fwd.wait_recv()
    for j in range(4):
        qt_audio[j] = qg[8 * j:8 * j + 8].reshape(256, WIDTH).T * BF16(0.125)

    def pass_copies(j):
        return (
            pltpu.make_async_remote_copy(
                src_ref=pass_o.at[j], dst_ref=got_o.at[j], send_sem=po_send.at[j],
                recv_sem=po_recv.at[j], device_id=sibling, device_id_type=MESH),
            pltpu.make_async_remote_copy(
                src_ref=pass_st.at[j], dst_ref=got_st.at[j], send_sem=ps_send.at[j],
                recv_sem=ps_recv.at[j], device_id=sibling, device_id_type=MESH))

    def ret_copies(s, device):
        return (
            pltpu.make_async_remote_copy(
                src_ref=ret_stage.at[s], dst_ref=ret_recv.at[s], send_sem=ret_send.at[s],
                recv_sem=ret_rsem.at[s], device_id=device, device_id_type=MESH),
            pltpu.make_async_remote_copy(
                src_ref=stat.at[s // 4], dst_ref=stat_recv.at[s], send_sem=st_send.at[s],
                recv_sem=st_rsem.at[s], device_id=device, device_id_type=MESH))

    def audio_heads(j, after, top, finish):
        steps = [(0, j, s_c), (1, j, s_d), (2, j, s_c), (3, j, s_d), (0, after, s_c)]
        for h in range(4):
            nh, nj, ns = steps[h + 1]
            top_h = top
            top, acc, total = both((video_keys, ROWS, qt_audio, nj, nh, ns) if nj is not None else None,
                                   (steps[h][2], top_h, vt_local, h, ROWS))
            finish(h, top_h, acc, total)
        return top

    def pass_chunk(j, top):
        def finish(h, top_h, acc, total):
            pass_o[j, h * HEAD_DIM:(h + 1) * HEAD_DIM, :] = acc.astype(BF16)
            pass_st[j, h:h + 1, :] = top_h
            pass_st[j, 4 + h:5 + h, :] = total

        top = audio_heads(2 + j, (3 + j) % 4, top, finish)
        for copy in pass_copies(j):
            copy.start()

        @pl.when(j == 0)
        def _():
            pass_on(1)
        return top

    top, _, _ = both((video_keys, ROWS, qt_audio, 2, 0, s_c), None)
    top = lax.fori_loop(0, 2, pass_chunk, top)

    for g in range(4):
        turn_values(1, g)
    for g in range(4):
        kv_fwd(1, g).wait_recv()
        turn_values(1, 4 + g)
    video_top = video_chunks(1, 0, BEFORE, None, video_start(1))

    for j in range(2):
        for copy in pass_copies(j):
            copy.wait_recv()

        def finish(h, top_h, acc, total, j=j):
            other_top = got_st[j, h:h + 1, :]
            peak = jnp.maximum(top_h, other_top)
            a = jnp.exp2((top_h - peak) * LOG2E)
            b = jnp.exp2((other_top - peak) * LOG2E)
            rows = slice(h * HEAD_DIM, (h + 1) * HEAD_DIM)
            o_t[rows, :] = acc * a + got_o[j, rows, :].astype(F32) * b
            norm = total * a + got_st[j, 4 + h:5 + h, :] * b
            for half in range(2):
                lanes = slice(half * 128, half * 128 + 128)
                stat[2 * j + half, h:h + 1, :] = peak[:, lanes]
                stat[2 * j + half, 4 + h:5 + h, :] = norm[:, lanes]

        top = audio_heads(j, 1 if j == 0 else None, top, finish)
        out = o_t[...].T.astype(BF16).reshape(8, AROWS, WIDTH)
        for p in range(8):
            s = 8 * j + p
            ret_stage[s] = out[p]
        for s in range(8 * j, 8 * j + 8):
            if s > 0:
                for copy in ret_copies(s, chip(s)):
                    copy.start()
    if BEFORE < 4:
        video_chunks(1, BEFORE, 4, None, video_top)
    ret_recv[0] = ret_stage[0]
    stat_recv[0] = stat[0]

    for pair in range(2):
        for d in range(1, NZ):
            z_copy(pair, d, slot_of(d)).wait_recv()

    def received(pair, d):
        return (stage[pair, slot_of(0)] if d == 0 else recv[pair, d]).astype(F32)

    total = None
    for pair in range(2):
        for d in range(NZ):
            wide = received(pair, d)
            part = jnp.sum(wide * wide, axis=1, keepdims=True)
            total = part if total is None else total + part
    factor = lax.rsqrt(total * (1.0 / (NZ * WIDTH)) + 1e-06)
    for d in range(NZ):
        for pair in range(2):
            column = pl.multiple_of(((z + NZ - d) % NZ) * WIDTH + 128 * pair, 128)
            lanes = pl.ds(column, 128)
            vout[:, lanes] = (received(pair, d) * factor * gain[:, lanes]).astype(BF16)

    for s in range(1, NC):
        for copy in ret_copies(s, chip(s)):
            copy.wait_recv()

    for s in range(1, NC):
        kv_copy(0, s).wait_send()
        kv_copy(1, s).wait_send()
        q_copy(s).wait_send()
    for g in range(4):
        kv_fwd(0, g).wait_send()
        kv_fwd(1, g).wait_send()
    q_fwd.wait_send()
    for d in range(1, NZ):
        z_copy(0, d, slot_of(d)).wait_send()
        z_copy(1, d, slot_of(d)).wait_send()
    for j in range(2):
        for copy in pass_copies(j):
            copy.wait_send()
    for s in range(1, NC):
        for copy in ret_copies(s, chip(s)):
            copy.wait_send()


def finish_kernel(rows, ret_recv, stat_recv, vout, aout, merged_buf, w_buf, sem):
    rows_out = pltpu.make_async_copy(rows, vout, sem.at[0])
    rows_out.start()
    tiles = []
    for s in range(NC):
        tile = stat_recv[s]
        shift = (128 - 32 * (s % 4)) % 128
        tiles.append(pltpu.roll(tile, shift, 1) if shift else tile)
    peak = tiles[0]
    for tile in tiles[1:]:
        peak = jnp.maximum(peak, tile)
    norm = None
    weights = []
    for tile in tiles:
        w = jnp.exp2((tile - peak) * LOG2E)
        weights.append(w)
        part = w * pltpu.roll(tile, 4, 0)
        norm = part if norm is None else norm + part
    for s in range(NC):
        w_buf[s] = weights[s] / norm
    turned = w_buf[...].reshape(NC * 8, 128).T[:AROWS]
    lane = lax.broadcasted_iota(jnp.int32, (AROWS, 128), 1)
    for pair in range(2):
        lanes = slice(pair * 128, pair * 128 + 128)
        merged = None
        for s in range(NC):
            at = s * 8 + 2 * pair
            w = jnp.where(lane < HEAD_DIM, turned[:, at:at + 1], turned[:, at + 1:at + 2])
            part = w * ret_recv[s, :, lanes].astype(F32)
            merged = part if merged is None else merged + part
        merged_buf[:, lanes] = merged.astype(BF16)
    merged_out = pltpu.make_async_copy(merged_buf, aout, sem.at[1])
    merged_out.start()
    merged_out.wait()
    rows_out.wait()


def shards(video_q, video_k, video_v, audio_q, audio_k, audio_v, norm_gain):
    arrays = (video_q, video_k, video_v, audio_q, audio_k, audio_v, norm_gain.reshape(1, -1))
    arrays = [pltpu.with_memory_space_constraint(a, pltpu.HBM) for a in arrays]
    vmem = pl.BlockSpec(memory_space=pltpu.VMEM)
    dma = pltpu.SemaphoreType.DMA
    rows, ret_recv, stat_recv = pl.pallas_call(
        kernel,
        out_shape=(
            jax.ShapeDtypeStruct((PIECE, NZ * WIDTH), BF16),
            jax.ShapeDtypeStruct((NC, AROWS, WIDTH), BF16),
            jax.ShapeDtypeStruct((NC, 8, 128), F32),
        ),
        in_specs=[pl.BlockSpec(memory_space=pltpu.HBM)] * 7,
        out_specs=(vmem, vmem, vmem),
        scratch_shapes=[
            pltpu.VMEM((1, NZ * WIDTH), F32),
            pltpu.VMEM((ROWS, WIDTH), BF16),
            pltpu.VMEM((ROWS, WIDTH), BF16),
            pltpu.VMEM((ROWS, WIDTH), BF16),
            pltpu.VMEM((4, WIDTH, 256), BF16),
            pltpu.VMEM((4, HEAD_DIM, ROWS), BF16),
            pltpu.VMEM((2, 2 * NC, 2, AROWS, 128), BF16),
            pltpu.VMEM((2 * NC, AROWS, WIDTH), BF16),
            pltpu.VMEM((4, HEAD_DIM, KEYS), BF16),
            pltpu.VMEM((4, WIDTH, 256), BF16),
            pltpu.VMEM((KEYS, 256), F32),
            pltpu.VMEM((KEYS, 256), F32),
            pltpu.VMEM((ROWS, 256), F32),
            pltpu.VMEM((ROWS, 256), F32),
            pltpu.VMEM((WIDTH, 256), F32),
            pltpu.VMEM((2, NZ, PIECE, 128), BF16),
            pltpu.VMEM((2, NZ, PIECE, 128), BF16),
            pltpu.VMEM((2, WIDTH, 256), BF16),
            pltpu.VMEM((2, 8, 256), F32),
            pltpu.VMEM((2, WIDTH, 256), BF16),
            pltpu.VMEM((2, 8, 256), F32),
            pltpu.VMEM((NC, AROWS, WIDTH), BF16),
            pltpu.VMEM((4, 8, 128), F32),
            dma((9,)), dma((2, NC)), dma((2, NC)), dma((NC,)), dma((NC,)), dma((2, 4)), dma((2, 4)),
            dma, dma, dma((2, NZ)), dma((2, NZ)), dma((2,)), dma((2,)), dma((2,)), dma((2,)),
            dma((NC,)), dma((NC,)), dma((NC,)), dma((NC,)),
        ],
        compiler_params=pltpu.CompilerParams(
            collective_id=0, has_side_effects=True, vmem_limit_bytes=24 * 1024 * 1024),
    )(*arrays)
    return pl.pallas_call(
        finish_kernel,
        out_shape=(
            jax.ShapeDtypeStruct((PIECE, NZ * WIDTH), BF16),
            jax.ShapeDtypeStruct((AROWS, WIDTH), BF16),
        ),
        in_specs=[vmem] * 3,
        out_specs=(pl.BlockSpec(memory_space=pltpu.HBM),) * 2,
        scratch_shapes=[
            pltpu.VMEM((AROWS, WIDTH), BF16),
            pltpu.VMEM((NC, 8, 128), F32),
            dma((2,)),
        ],
        compiler_params=pltpu.CompilerParams(vmem_limit_bytes=4 * 1024 * 1024),
    )(rows, ret_recv, stat_recv)


def solution(mesh):
    placed = P("tok", "head")
    return jax.shard_map(
        shards,
        mesh=mesh,
        in_specs=(placed,) * 6 + (P(),),
        out_specs=(P(("tok", "head"), None), placed),
        check_vma=False,
    )
```

```python
import jax
import jax.numpy as jnp
from jax import lax
from jax.experimental import pallas as pl
from jax.experimental.pallas import tpu as pltpu
from jax.sharding import PartitionSpec as P

MESH = pl.DeviceIdType.MESH
F32, BF16 = jnp.float32, jnp.bfloat16
HEAD_DIM = 64
LOG2E = 1.4426950408889634
NZ = 8
NC = 16
ROWS = 896
PIECE = 112
AROWS = 32
WIDTH = 256
KEYS = 1024
BLOCK = 512
BEFORE = 2

CHIPS = sorted(((dx, dy) for dx in range(4) for dy in range(4)),
               key=lambda d: -(min(d[0], 4 - d[0]) + min(d[1], 4 - d[1])))
CHIPS = CHIPS[-1:] + CHIPS[:-1]


def key_blocks(count):
    return [(start, min(BLOCK, count - start)) for start in range(0, count, BLOCK)]


def slot_of(d):
    if d == 0:
        return 1
    return 2 * (4 - d) if d <= 4 else 2 * (d - 4) + 1


def loop(start, stop, body):
    def step(i, carry):
        body(i)
        return carry
    lax.fori_loop(start, stop, step, 0)


def kernel(vq, vk, vv, aq, ak, av, gain_hbm, vout, ret_recv, stat_recv,
           gain, q_buf, k_buf, v_buf, qt, vt_local, kvg, qg, vt_audio, qt_audio,
           s_a, s_b, s_c, s_d, o_t, stage, recv, pass_o, pass_st, got_o, got_st,
           ret_stage, stat,
           in_sem, kv_send, kv_recv, q_send, q_recv, fwd_send, fwd_recv, qf_send, qf_recv,
           z_send, z_recv, po_send, po_recv, ps_send, ps_recv,
           ret_send, ret_rsem, st_send, st_rsem):
    z = lax.axis_index("head")
    t = lax.axis_index("tok")
    x, y, c = t // 8, (t // 2) % 4, t % 2
    xs = [((x + i) % 4) * 8 + c for i in range(4)]
    ys = [((y + i) % 4) * 2 for i in range(4)]
    zs = [(z + i) % NZ for i in range(NZ)]
    sibling = (z, t + 1 - 2 * c)

    def chip(s, sign=1):
        dx, dy = CHIPS[s]
        return (z, xs[sign * dx % 4] + ys[sign * dy % 4])

    barrier = pltpu.get_barrier_semaphore()
    peers = [(min(d, NZ - d), (zs[d], t)) for d in range(1, NZ)]
    peers += [(min(CHIPS[i][0], 4 - CHIPS[i][0]) + min(CHIPS[i][1], 4 - CHIPS[i][1]), chip(i))
              for i in range(1, NC)]
    for _, device in sorted(peers, key=lambda peer: -peer[0]) + [(0, sibling)]:
        pl.semaphore_signal(barrier, inc=1, device_id=device, device_id_type=MESH)

    own = [
        pltpu.make_async_copy(src, dst, in_sem.at[i]) for i, (src, dst) in enumerate([
            (ak.at[:, 0:128], kvg.at[0, 0, 0]), (av.at[:, 0:128], kvg.at[0, 0, 1]),
            (ak.at[:, 128:256], kvg.at[1, 0, 0]), (av.at[:, 128:256], kvg.at[1, 0, 1]),
            (aq, qg.at[0]), (vq, q_buf), (vv, v_buf), (vk, k_buf), (gain_hbm, gain)])
    ]
    for copy in own:
        copy.start()

    for copy in own[:5]:
        copy.wait()
    pl.semaphore_wait(barrier, NZ - 1 + NC)

    def kv_copy(pair, s):
        return pltpu.make_async_remote_copy(
            src_ref=kvg.at[pair, 0], dst_ref=kvg.at[pair, s], send_sem=kv_send.at[pair, s],
            recv_sem=kv_recv.at[pair, s], device_id=chip(s, -1), device_id_type=MESH)

    def q_copy(s):
        return pltpu.make_async_remote_copy(
            src_ref=qg.at[0], dst_ref=qg.at[s], send_sem=q_send.at[s], recv_sem=q_recv.at[s],
            device_id=chip(s, -1), device_id_type=MESH)

    for s in range(1, NC):
        kv_copy(0, s).start()
    for s in range(1, NC):
        q_copy(s).start()
    for s in range(1, NC):
        kv_copy(1, s).start()

    own[5].wait()
    for j in range(4):
        parts = []
        for d in (4 - j, 4 + j if j else 0):
            start = pl.multiple_of(zs[d] * PIECE, 16)
            parts.append(q_buf[pl.ds(start, PIECE), :])
            parts.append(jnp.zeros((128 - PIECE, WIDTH), BF16))
        qt[j] = jnp.concatenate(parts, axis=0).T * BF16(0.125)
    own[6].wait()
    for start in range(0, ROWS, 128):
        turned = v_buf[start:start + 128, :].T
        for h in range(4):
            vt_local[h, :, start:start + 128] = turned[h * HEAD_DIM:(h + 1) * HEAD_DIM]
    own[7].wait()
    own[8].wait()

    def kv_fwd(pair, g):
        return pltpu.make_async_remote_copy(
            src_ref=kvg.at[pair, 4 * g:4 * g + 4], dst_ref=kvg.at[pair, NC + 4 * g:NC + 4 * g + 4],
            send_sem=fwd_send.at[pair, g], recv_sem=fwd_recv.at[pair, g], device_id=sibling,
            device_id_type=MESH)

    def turn_values(pair, g):
        turned = kvg[pair, 4 * g:4 * g + 4, 1].reshape(128, 128).T
        for h in range(2):
            vt_audio[2 * pair + h, :, g * 128:g * 128 + 128] = turned[h * HEAD_DIM:(h + 1) * HEAD_DIM]

    def pass_on(pair):
        for g in range(4):
            for s in range(max(4 * g, 1), 4 * g + 4):
                kv_copy(pair, s).wait_recv()
            kv_fwd(pair, g).start()

    pass_on(0)
    for g in range(4):
        turn_values(0, g)
    for g in range(4):
        kv_fwd(0, g).wait_recv()
        turn_values(0, 4 + g)

    q_fwd = pltpu.make_async_remote_copy(
        src_ref=qg.at[0:NC], dst_ref=qg.at[NC:2 * NC], send_sem=qf_send, recv_sem=qf_recv,
        device_id=sibling, device_id_type=MESH)

    row = lax.broadcasted_iota(jnp.int32, (128, 256), 0)

    def masked(qt_ref, j, h):
        pair = qt_ref[j, (h // 2) * 128:(h // 2) * 128 + 128, :]
        keep = (row < HEAD_DIM) if h % 2 == 0 else (row >= HEAD_DIM)
        return jnp.where(keep, pair, jnp.zeros_like(pair))

    def audio_keys(start, size, h):
        return kvg[h // 2, start // 32:(start + size) // 32, 0].reshape(size, 128)

    def video_keys(start, size, h):
        return k_buf[start:start + size, (h // 2) * 128:(h // 2) * 128 + 128]

    def both(first, second):
        top, acc, total = None, None, None
        if first is not None:
            keys, count, qt_ref, j, h, s_out = first
            q_head = masked(qt_ref, j, h)
        if second is not None:
            s_in, top_in, vt_ref, h_in, count = second
        for start, size in key_blocks(count):
            if first is not None:
                s = jnp.dot(keys(start, size, h), q_head, preferred_element_type=F32)
                s_out[start:start + size, :] = s
                part = jnp.max(s.reshape(size // 8, 8, 256), axis=0)
                top = part if top is None else jnp.maximum(top, part)
            if second is not None:
                w = jnp.exp2((s_in[start:start + size, :] - top_in) * LOG2E)
                part = jnp.sum(w.reshape(size // 8, 8, 256), axis=0)
                total = part if total is None else total + part
                o = jnp.dot(vt_ref[h_in, :, start:start + size], w.astype(BF16),
                            preferred_element_type=F32)
                acc = o if acc is None else acc + o
        if top is not None:
            top = jnp.max(top, axis=0, keepdims=True)
        if total is not None:
            total = jnp.sum(total, axis=0, keepdims=True)
        return top, acc, total

    def z_copy(pair, d, slot):
        return pltpu.make_async_remote_copy(
            src_ref=stage.at[pair, slot], dst_ref=recv.at[pair, d], send_sem=z_send.at[pair, d],
            recv_sem=z_recv.at[pair, d], device_id=((z + d) % NZ, t), device_id_type=MESH)

    def video_chunk(pair, at_one, j, top, last=False):
        after = jnp.minimum(j + 1, 3)
        h0, h1 = 2 * pair, 2 * pair + 1
        top, acc, total = both((audio_keys, KEYS, qt, j, h1, s_b), (s_a, top, vt_audio, h0, KEYS))
        o_t[:HEAD_DIM, :] = acc / total
        top, acc, total = both(None if last else (audio_keys, KEYS, qt, after, h0, s_a),
                               (s_b, top, vt_audio, h1, KEYS))
        o_t[HEAD_DIM:2 * HEAD_DIM, :] = acc / total
        out = o_t[:2 * HEAD_DIM, :].T.astype(BF16)
        stage[pair, 2 * j] = out[:PIECE]
        stage[pair, 2 * j + 1] = out[128:128 + PIECE]
        z_copy(pair, 4 - j, 2 * j).start()

        @pl.when(j > 0)
        def _():
            z_copy(pair, 4 + j, 2 * j + 1).start()

        if at_one is not None:
            pl.when(j == 1)(at_one)
        return top

    def video_start(pair):
        return both((audio_keys, KEYS, qt, 0, 2 * pair, s_a), None)[0]

    def video_chunks(pair, start, stop, at_one, top):
        top = lax.fori_loop(start, min(stop, 3), lambda j, top: video_chunk(pair, at_one, j, top), top)
        return video_chunk(pair, None, jnp.int32(3), top, last=True) if stop == 4 else top

    def pass_queries():
        for s in range(1, NC):
            q_copy(s).wait_recv()
        q_fwd.start()

    video_chunks(0, 0, 4, pass_queries, video_start(0))

    q_fwd.wait_recv()
    for j in range(4):
        qt_audio[j] = qg[8 * j:8 * j + 8].reshape(256, WIDTH).T * BF16(0.125)

    def pass_copies(j):
        return (
            pltpu.make_async_remote_copy(
                src_ref=pass_o.at[j], dst_ref=got_o.at[j], send_sem=po_send.at[j],
                recv_sem=po_recv.at[j], device_id=sibling, device_id_type=MESH),
            pltpu.make_async_remote_copy(
                src_ref=pass_st.at[j], dst_ref=got_st.at[j], send_sem=ps_send.at[j],
                recv_sem=ps_recv.at[j], device_id=sibling, device_id_type=MESH))

    def ret_copies(s, device):
        return (
            pltpu.make_async_remote_copy(
                src_ref=ret_stage.at[s], dst_ref=ret_recv.at[s], send_sem=ret_send.at[s],
                recv_sem=ret_rsem.at[s], device_id=device, device_id_type=MESH),
            pltpu.make_async_remote_copy(
                src_ref=stat.at[s // 4], dst_ref=stat_recv.at[s], send_sem=st_send.at[s],
                recv_sem=st_rsem.at[s], device_id=device, device_id_type=MESH))

    def audio_heads(j, after, top, finish):
        steps = [(0, j, s_c), (1, j, s_d), (2, j, s_c), (3, j, s_d), (0, after, s_c)]
        for h in range(4):
            nh, nj, ns = steps[h + 1]
            top_h = top
            top, acc, total = both((video_keys, ROWS, qt_audio, nj, nh, ns) if nj is not None else None,
                                   (steps[h][2], top_h, vt_local, h, ROWS))
            finish(h, top_h, acc, total)
        return top

    def pass_chunk(j, top):
        def finish(h, top_h, acc, total):
            pass_o[j, h * HEAD_DIM:(h + 1) * HEAD_DIM, :] = acc.astype(BF16)
            pass_st[j, h:h + 1, :] = top_h
            pass_st[j, 4 + h:5 + h, :] = total

        top = audio_heads(2 + j, (3 + j) % 4, top, finish)
        for copy in pass_copies(j):
            copy.start()

        @pl.when(j == 0)
        def _():
            pass_on(1)
        return top

    top, _, _ = both((video_keys, ROWS, qt_audio, 2, 0, s_c), None)
    top = lax.fori_loop(0, 2, pass_chunk, top)

    for g in range(4):
        turn_values(1, g)
    for g in range(4):
        kv_fwd(1, g).wait_recv()
        turn_values(1, 4 + g)
    video_top = video_chunks(1, 0, BEFORE, None, video_start(1))

    for j in range(2):
        for copy in pass_copies(j):
            copy.wait_recv()

        def finish(h, top_h, acc, total, j=j):
            other_top = got_st[j, h:h + 1, :]
            peak = jnp.maximum(top_h, other_top)
            a = jnp.exp2((top_h - peak) * LOG2E)
            b = jnp.exp2((other_top - peak) * LOG2E)
            rows = slice(h * HEAD_DIM, (h + 1) * HEAD_DIM)
            o_t[rows, :] = acc * a + got_o[j, rows, :].astype(F32) * b
            norm = total * a + got_st[j, 4 + h:5 + h, :] * b
            for half in range(2):
                lanes = slice(half * 128, half * 128 + 128)
                stat[2 * j + half, h:h + 1, :] = peak[:, lanes]
                stat[2 * j + half, 4 + h:5 + h, :] = norm[:, lanes]

        top = audio_heads(j, 1 if j == 0 else None, top, finish)
        out = o_t[...].T.astype(BF16).reshape(8, AROWS, WIDTH)
        for p in range(8):
            s = 8 * j + p
            ret_stage[s] = out[p]
        for s in range(8 * j, 8 * j + 8):
            if s > 0:
                for copy in ret_copies(s, chip(s)):
                    copy.start()
    if BEFORE < 4:
        video_chunks(1, BEFORE, 4, None, video_top)
    ret_recv[0] = ret_stage[0]
    stat_recv[0] = stat[0]

    def received(pair, d):
        return (stage[pair, slot_of(0)] if d == 0 else recv[pair, d]).astype(F32)

    total = None
    for pair in range(2):
        for d in range(1, NZ):
            z_copy(pair, d, slot_of(d)).wait_recv()
        for d in range(NZ):
            wide = received(pair, d)
            part = jnp.sum(wide * wide, axis=1, keepdims=True)
            total = part if total is None else total + part
    factor = lax.rsqrt(total * (1.0 / (NZ * WIDTH)) + 1e-06)
    for d in range(NZ):
        for pair in range(2):
            column = pl.multiple_of(((z + NZ - d) % NZ) * WIDTH + 128 * pair, 128)
            lanes = pl.ds(column, 128)
            vout[:, lanes] = (received(pair, d) * factor * gain[:, lanes]).astype(BF16)

    for s in range(1, NC):
        for copy in ret_copies(s, chip(s)):
            copy.wait_recv()

    for s in range(1, NC):
        kv_copy(0, s).wait_send()
        kv_copy(1, s).wait_send()
        q_copy(s).wait_send()
    for g in range(4):
        kv_fwd(0, g).wait_send()
        kv_fwd(1, g).wait_send()
    q_fwd.wait_send()
    for d in range(1, NZ):
        z_copy(0, d, slot_of(d)).wait_send()
        z_copy(1, d, slot_of(d)).wait_send()
    for j in range(2):
        for copy in pass_copies(j):
            copy.wait_send()
    for s in range(1, NC):
        for copy in ret_copies(s, chip(s)):
            copy.wait_send()


def finish_kernel(rows, ret_recv, stat_recv, vout, aout, merged_buf, w_buf, sem):
    rows_out = pltpu.make_async_copy(rows, vout, sem.at[0])
    rows_out.start()
    tiles = []
    for s in range(NC):
        tile = stat_recv[s]
        shift = (128 - 32 * (s % 4)) % 128
        tiles.append(pltpu.roll(tile, shift, 1) if shift else tile)
    peak = tiles[0]
    for tile in tiles[1:]:
        peak = jnp.maximum(peak, tile)
    norm = None
    weights = []
    for tile in tiles:
        w = jnp.exp2((tile - peak) * LOG2E)
        weights.append(w)
        part = w * pltpu.roll(tile, 4, 0)
        norm = part if norm is None else norm + part
    for s in range(NC):
        w_buf[s] = weights[s] / norm
    turned = w_buf[...].reshape(NC * 8, 128).T[:AROWS]
    lane = lax.broadcasted_iota(jnp.int32, (AROWS, 128), 1)
    for pair in range(2):
        lanes = slice(pair * 128, pair * 128 + 128)
        merged = None
        for s in range(NC):
            at = s * 8 + 2 * pair
            w = jnp.where(lane < HEAD_DIM, turned[:, at:at + 1], turned[:, at + 1:at + 2])
            part = w * ret_recv[s, :, lanes].astype(F32)
            merged = part if merged is None else merged + part
        merged_buf[:, lanes] = merged.astype(BF16)
    merged_out = pltpu.make_async_copy(merged_buf, aout, sem.at[1])
    merged_out.start()
    merged_out.wait()
    rows_out.wait()


def shards(video_q, video_k, video_v, audio_q, audio_k, audio_v, norm_gain):
    arrays = (video_q, video_k, video_v, audio_q, audio_k, audio_v, norm_gain.reshape(1, -1))
    arrays = [pltpu.with_memory_space_constraint(a, pltpu.HBM) for a in arrays]
    vmem = pl.BlockSpec(memory_space=pltpu.VMEM)
    dma = pltpu.SemaphoreType.DMA
    rows, ret_recv, stat_recv = pl.pallas_call(
        kernel,
        out_shape=(
            jax.ShapeDtypeStruct((PIECE, NZ * WIDTH), BF16),
            jax.ShapeDtypeStruct((NC, AROWS, WIDTH), BF16),
            jax.ShapeDtypeStruct((NC, 8, 128), F32),
        ),
        in_specs=[pl.BlockSpec(memory_space=pltpu.HBM)] * 7,
        out_specs=(vmem, vmem, vmem),
        scratch_shapes=[
            pltpu.VMEM((1, NZ * WIDTH), F32),
            pltpu.VMEM((ROWS, WIDTH), BF16),
            pltpu.VMEM((ROWS, WIDTH), BF16),
            pltpu.VMEM((ROWS, WIDTH), BF16),
            pltpu.VMEM((4, WIDTH, 256), BF16),
            pltpu.VMEM((4, HEAD_DIM, ROWS), BF16),
            pltpu.VMEM((2, 2 * NC, 2, AROWS, 128), BF16),
            pltpu.VMEM((2 * NC, AROWS, WIDTH), BF16),
            pltpu.VMEM((4, HEAD_DIM, KEYS), BF16),
            pltpu.VMEM((4, WIDTH, 256), BF16),
            pltpu.VMEM((KEYS, 256), F32),
            pltpu.VMEM((KEYS, 256), F32),
            pltpu.VMEM((ROWS, 256), F32),
            pltpu.VMEM((ROWS, 256), F32),
            pltpu.VMEM((WIDTH, 256), F32),
            pltpu.VMEM((2, NZ, PIECE, 128), BF16),
            pltpu.VMEM((2, NZ, PIECE, 128), BF16),
            pltpu.VMEM((2, WIDTH, 256), BF16),
            pltpu.VMEM((2, 8, 256), F32),
            pltpu.VMEM((2, WIDTH, 256), BF16),
            pltpu.VMEM((2, 8, 256), F32),
            pltpu.VMEM((NC, AROWS, WIDTH), BF16),
            pltpu.VMEM((4, 8, 128), F32),
            dma((9,)), dma((2, NC)), dma((2, NC)), dma((NC,)), dma((NC,)), dma((2, 4)), dma((2, 4)),
            dma, dma, dma((2, NZ)), dma((2, NZ)), dma((2,)), dma((2,)), dma((2,)), dma((2,)),
            dma((NC,)), dma((NC,)), dma((NC,)), dma((NC,)),
        ],
        compiler_params=pltpu.CompilerParams(
            collective_id=0, has_side_effects=True, vmem_limit_bytes=24 * 1024 * 1024),
    )(*arrays)
    return pl.pallas_call(
        finish_kernel,
        out_shape=(
            jax.ShapeDtypeStruct((PIECE, NZ * WIDTH), BF16),
            jax.ShapeDtypeStruct((AROWS, WIDTH), BF16),
        ),
        in_specs=[vmem] * 3,
        out_specs=(pl.BlockSpec(memory_space=pltpu.HBM),) * 2,
        scratch_shapes=[
            pltpu.VMEM((AROWS, WIDTH), BF16),
            pltpu.VMEM((NC, 8, 128), F32),
            dma((2,)),
        ],
        compiler_params=pltpu.CompilerParams(vmem_limit_bytes=4 * 1024 * 1024),
    )(rows, ret_recv, stat_recv)


def solution(mesh):
    placed = P("tok", "head")
    return jax.shard_map(
        shards,
        mesh=mesh,
        in_specs=(placed,) * 6 + (P(),),
        out_specs=(P(("tok", "head"), None), placed),
        check_vma=False,
    )
```

```python
import jax
import jax.numpy as jnp
from jax import lax
from jax.experimental import pallas as pl
from jax.experimental.pallas import tpu as pltpu
from jax.sharding import PartitionSpec as P

MESH = pl.DeviceIdType.MESH
F32, BF16 = jnp.float32, jnp.bfloat16
HEAD_DIM = 64
LOG2E = 1.4426950408889634
NZ = 8
NC = 16
ROWS = 896
PIECE = 112
AROWS = 32
WIDTH = 256
KEYS = 1024
BLOCK = 512
BEFORE = 2

CHIPS = sorted(((dx, dy) for dx in range(4) for dy in range(4)),
               key=lambda d: -(min(d[0], 4 - d[0]) + min(d[1], 4 - d[1])))
CHIPS = CHIPS[-1:] + CHIPS[:-1]


def key_blocks(count):
    return [(start, min(BLOCK, count - start)) for start in range(0, count, BLOCK)]


def slot_of(d):
    if d == 0:
        return 1
    return 2 * (4 - d) if d <= 4 else 2 * (d - 4) + 1


def loop(start, stop, body):
    def step(i, carry):
        body(i)
        return carry
    lax.fori_loop(start, stop, step, 0)


def kernel(vq, vk, vv, aq, ak, av, gain_hbm, vout, ret_recv, stat_recv,
           gain, q_buf, k_buf, v_buf, qt, vt_local, kvg, qg, vt_audio, qt_audio,
           s_a, s_b, s_c, s_d, o_t, stage, recv, pass_o, pass_st, got_o, got_st,
           ret_stage, stat,
           in_sem, kv_send, kv_recv, q_send, q_recv, fwd_send, fwd_recv, qf_send, qf_recv,
           z_send, z_recv, po_send, po_recv, ps_send, ps_recv,
           ret_send, ret_rsem, st_send, st_rsem):
    z = lax.axis_index("head")
    t = lax.axis_index("tok")
    x, y, c = t // 8, (t // 2) % 4, t % 2
    xs = [((x + i) % 4) * 8 + c for i in range(4)]
    ys = [((y + i) % 4) * 2 for i in range(4)]
    zs = [(z + i) % NZ for i in range(NZ)]
    sibling = (z, t + 1 - 2 * c)

    def chip(s, sign=1):
        dx, dy = CHIPS[s]
        return (z, xs[sign * dx % 4] + ys[sign * dy % 4])

    barrier = pltpu.get_barrier_semaphore()
    peers = [(min(d, NZ - d), (zs[d], t)) for d in range(1, NZ)]
    peers += [(min(CHIPS[i][0], 4 - CHIPS[i][0]) + min(CHIPS[i][1], 4 - CHIPS[i][1]), chip(i))
              for i in range(1, NC)]
    for _, device in sorted(peers, key=lambda peer: -peer[0]) + [(0, sibling)]:
        pl.semaphore_signal(barrier, inc=1, device_id=device, device_id_type=MESH)

    own = [
        pltpu.make_async_copy(src, dst, in_sem.at[i]) for i, (src, dst) in enumerate([
            (ak.at[:, 0:128], kvg.at[0, 0, 0]), (av.at[:, 0:128], kvg.at[0, 0, 1]),
            (ak.at[:, 128:256], kvg.at[1, 0, 0]), (av.at[:, 128:256], kvg.at[1, 0, 1]),
            (aq, qg.at[0]), (vq, q_buf), (vv, v_buf), (vk, k_buf), (gain_hbm, gain)])
    ]
    for copy in own:
        copy.start()

    for copy in own[:5]:
        copy.wait()
    pl.semaphore_wait(barrier, NZ - 1 + NC)

    def kv_copy(pair, s):
        return pltpu.make_async_remote_copy(
            src_ref=kvg.at[pair, 0], dst_ref=kvg.at[pair, s], send_sem=kv_send.at[pair, s],
            recv_sem=kv_recv.at[pair, s], device_id=chip(s, -1), device_id_type=MESH)

    def q_copy(s):
        return pltpu.make_async_remote_copy(
            src_ref=qg.at[0], dst_ref=qg.at[s], send_sem=q_send.at[s], recv_sem=q_recv.at[s],
            device_id=chip(s, -1), device_id_type=MESH)

    for s in range(1, NC):
        kv_copy(0, s).start()
    for s in range(1, NC):
        q_copy(s).start()
    for s in range(1, NC):
        kv_copy(1, s).start()

    own[5].wait()
    for j in range(4):
        parts = []
        for d in (4 - j, 4 + j if j else 0):
            start = pl.multiple_of(zs[d] * PIECE, 16)
            parts.append(q_buf[pl.ds(start, PIECE), :])
            parts.append(jnp.zeros((128 - PIECE, WIDTH), BF16))
        qt[j] = jnp.concatenate(parts, axis=0).T * BF16(0.125)
    own[6].wait()
    for start in range(0, ROWS, 128):
        turned = v_buf[start:start + 128, :].T
        for h in range(4):
            vt_local[h, :, start:start + 128] = turned[h * HEAD_DIM:(h + 1) * HEAD_DIM]
    own[7].wait()
    own[8].wait()

    def kv_fwd(pair, g):
        return pltpu.make_async_remote_copy(
            src_ref=kvg.at[pair, 4 * g:4 * g + 4], dst_ref=kvg.at[pair, NC + 4 * g:NC + 4 * g + 4],
            send_sem=fwd_send.at[pair, g], recv_sem=fwd_recv.at[pair, g], device_id=sibling,
            device_id_type=MESH)

    def turn_values(pair, g):
        turned = kvg[pair, 4 * g:4 * g + 4, 1].reshape(128, 128).T
        for h in range(2):
            vt_audio[2 * pair + h, :, g * 128:g * 128 + 128] = turned[h * HEAD_DIM:(h + 1) * HEAD_DIM]

    def pass_on(pair):
        for g in range(4):
            for s in range(max(4 * g, 1), 4 * g + 4):
                kv_copy(pair, s).wait_recv()
            kv_fwd(pair, g).start()

    pass_on(0)
    for g in range(4):
        turn_values(0, g)

    q_fwd = pltpu.make_async_remote_copy(
        src_ref=qg.at[0:NC], dst_ref=qg.at[NC:2 * NC], send_sem=qf_send, recv_sem=qf_recv,
        device_id=sibling, device_id_type=MESH)

    row = lax.broadcasted_iota(jnp.int32, (128, 256), 0)

    def masked(qt_ref, j, h):
        pair = qt_ref[j, (h // 2) * 128:(h // 2) * 128 + 128, :]
        keep = (row < HEAD_DIM) if h % 2 == 0 else (row >= HEAD_DIM)
        return jnp.where(keep, pair, jnp.zeros_like(pair))

    def audio_keys(start, size, h):
        return kvg[h // 2, start // 32:(start + size) // 32, 0].reshape(size, 128)

    def video_keys(start, size, h):
        return k_buf[start:start + size, (h // 2) * 128:(h // 2) * 128 + 128]

    def both(first, second):
        top, acc, total = None, None, None
        if first is not None:
            keys, count, qt_ref, j, h, s_out = first
            q_head = masked(qt_ref, j, h)
        if second is not None:
            s_in, top_in, vt_ref, h_in, count = second
        for start, size in key_blocks(count):
            if first is not None:
                s = jnp.dot(keys(start, size, h), q_head, preferred_element_type=F32)
                s_out[start:start + size, :] = s
                part = jnp.max(s.reshape(size // 8, 8, 256), axis=0)
                top = part if top is None else jnp.maximum(top, part)
            if second is not None:
                w = jnp.exp2((s_in[start:start + size, :] - top_in) * LOG2E)
                part = jnp.sum(w.reshape(size // 8, 8, 256), axis=0)
                total = part if total is None else total + part
                o = jnp.dot(vt_ref[h_in, :, start:start + size], w.astype(BF16),
                            preferred_element_type=F32)
                acc = o if acc is None else acc + o
        if top is not None:
            top = jnp.max(top, axis=0, keepdims=True)
        if total is not None:
            total = jnp.sum(total, axis=0, keepdims=True)
        return top, acc, total

    def z_copy(pair, d, slot):
        return pltpu.make_async_remote_copy(
            src_ref=stage.at[pair, slot], dst_ref=recv.at[pair, d], send_sem=z_send.at[pair, d],
            recv_sem=z_recv.at[pair, d], device_id=((z + d) % NZ, t), device_id_type=MESH)

    def video_chunk(pair, at_one, j, top, last=False):
        after = jnp.minimum(j + 1, 3)
        h0, h1 = 2 * pair, 2 * pair + 1
        top, acc, total = both((audio_keys, KEYS, qt, j, h1, s_b), (s_a, top, vt_audio, h0, KEYS))
        o_t[:HEAD_DIM, :] = acc / total
        top, acc, total = both(None if last else (audio_keys, KEYS, qt, after, h0, s_a),
                               (s_b, top, vt_audio, h1, KEYS))
        o_t[HEAD_DIM:2 * HEAD_DIM, :] = acc / total
        out = o_t[:2 * HEAD_DIM, :].T.astype(BF16)
        stage[pair, 2 * j] = out[:PIECE]
        stage[pair, 2 * j + 1] = out[128:128 + PIECE]
        z_copy(pair, 4 - j, 2 * j).start()

        @pl.when(j > 0)
        def _():
            z_copy(pair, 4 + j, 2 * j + 1).start()

        if at_one is not None:
            pl.when(j == 1)(at_one)
        return top

    def video_start(pair):
        q_head = masked(qt, 0, 2 * pair)
        tops = []
        for start in (0, BLOCK):
            if start:
                for g in range(4):
                    kv_fwd(pair, g).wait_recv()
                    turn_values(pair, 4 + g)
            s = jnp.dot(audio_keys(start, BLOCK, 2 * pair), q_head, preferred_element_type=F32)
            s_a[start:start + BLOCK, :] = s
            tops.append(jnp.max(s, axis=0, keepdims=True))
        return jnp.maximum(*tops)

    def video_chunks(pair, start, stop, at_one, top):
        top = lax.fori_loop(start, min(stop, 3), lambda j, top: video_chunk(pair, at_one, j, top), top)
        return video_chunk(pair, None, jnp.int32(3), top, last=True) if stop == 4 else top

    def pass_queries():
        for s in range(1, NC):
            q_copy(s).wait_recv()
        q_fwd.start()

    video_chunks(0, 0, 4, pass_queries, video_start(0))

    q_fwd.wait_recv()
    for j in range(4):
        qt_audio[j] = qg[8 * j:8 * j + 8].reshape(256, WIDTH).T * BF16(0.125)

    def pass_copies(j):
        return (
            pltpu.make_async_remote_copy(
                src_ref=pass_o.at[j], dst_ref=got_o.at[j], send_sem=po_send.at[j],
                recv_sem=po_recv.at[j], device_id=sibling, device_id_type=MESH),
            pltpu.make_async_remote_copy(
                src_ref=pass_st.at[j], dst_ref=got_st.at[j], send_sem=ps_send.at[j],
                recv_sem=ps_recv.at[j], device_id=sibling, device_id_type=MESH))

    def ret_copies(s, device):
        return (
            pltpu.make_async_remote_copy(
                src_ref=ret_stage.at[s], dst_ref=ret_recv.at[s], send_sem=ret_send.at[s],
                recv_sem=ret_rsem.at[s], device_id=device, device_id_type=MESH),
            pltpu.make_async_remote_copy(
                src_ref=stat.at[s // 4], dst_ref=stat_recv.at[s], send_sem=st_send.at[s],
                recv_sem=st_rsem.at[s], device_id=device, device_id_type=MESH))

    def audio_heads(j, after, top, finish):
        steps = [(0, j, s_c), (1, j, s_d), (2, j, s_c), (3, j, s_d), (0, after, s_c)]
        for h in range(4):
            nh, nj, ns = steps[h + 1]
            top_h = top
            top, acc, total = both((video_keys, ROWS, qt_audio, nj, nh, ns) if nj is not None else None,
                                   (steps[h][2], top_h, vt_local, h, ROWS))
            finish(h, top_h, acc, total)
        return top

    def pass_chunk(j, top):
        def finish(h, top_h, acc, total):
            pass_o[j, h * HEAD_DIM:(h + 1) * HEAD_DIM, :] = acc.astype(BF16)
            pass_st[j, h:h + 1, :] = top_h
            pass_st[j, 4 + h:5 + h, :] = total

        top = audio_heads(2 + j, (3 + j) % 4, top, finish)
        for copy in pass_copies(j):
            copy.start()

        @pl.when(j == 0)
        def _():
            pass_on(1)
        return top

    top, _, _ = both((video_keys, ROWS, qt_audio, 2, 0, s_c), None)
    top = lax.fori_loop(0, 2, pass_chunk, top)

    for g in range(4):
        turn_values(1, g)
    video_top = video_chunks(1, 0, BEFORE, None, video_start(1))

    for j in range(2):
        for copy in pass_copies(j):
            copy.wait_recv()

        def finish(h, top_h, acc, total, j=j):
            other_top = got_st[j, h:h + 1, :]
            peak = jnp.maximum(top_h, other_top)
            a = jnp.exp2((top_h - peak) * LOG2E)
            b = jnp.exp2((other_top - peak) * LOG2E)
            rows = slice(h * HEAD_DIM, (h + 1) * HEAD_DIM)
            o_t[rows, :] = acc * a + got_o[j, rows, :].astype(F32) * b
            norm = total * a + got_st[j, 4 + h:5 + h, :] * b
            for half in range(2):
                lanes = slice(half * 128, half * 128 + 128)
                stat[2 * j + half, h:h + 1, :] = peak[:, lanes]
                stat[2 * j + half, 4 + h:5 + h, :] = norm[:, lanes]

        top = audio_heads(j, 1 if j == 0 else None, top, finish)
        out = o_t[...].T.astype(BF16).reshape(8, AROWS, WIDTH)
        for p in range(8):
            s = 8 * j + p
            ret_stage[s] = out[p]
        for s in range(8 * j, 8 * j + 8):
            if s > 0:
                for copy in ret_copies(s, chip(s)):
                    copy.start()
    if BEFORE < 4:
        video_chunks(1, BEFORE, 4, None, video_top)
    ret_recv[0] = ret_stage[0]
    stat_recv[0] = stat[0]

    def received(pair, d):
        return (stage[pair, slot_of(0)] if d == 0 else recv[pair, d]).astype(F32)

    total = None
    for pair in range(2):
        for d in range(1, NZ):
            z_copy(pair, d, slot_of(d)).wait_recv()
        for d in range(NZ):
            wide = received(pair, d)
            part = jnp.sum(wide * wide, axis=1, keepdims=True)
            total = part if total is None else total + part
    factor = lax.rsqrt(total * (1.0 / (NZ * WIDTH)) + 1e-06)
    for d in range(NZ):
        for pair in range(2):
            column = pl.multiple_of(((z + NZ - d) % NZ) * WIDTH + 128 * pair, 128)
            lanes = pl.ds(column, 128)
            vout[:, lanes] = (received(pair, d) * factor * gain[:, lanes]).astype(BF16)

    for s in range(1, NC):
        for copy in ret_copies(s, chip(s)):
            copy.wait_recv()

    for s in range(1, NC):
        kv_copy(0, s).wait_send()
        kv_copy(1, s).wait_send()
        q_copy(s).wait_send()
    for g in range(4):
        kv_fwd(0, g).wait_send()
        kv_fwd(1, g).wait_send()
    q_fwd.wait_send()
    for d in range(1, NZ):
        z_copy(0, d, slot_of(d)).wait_send()
        z_copy(1, d, slot_of(d)).wait_send()
    for j in range(2):
        for copy in pass_copies(j):
            copy.wait_send()
    for s in range(1, NC):
        for copy in ret_copies(s, chip(s)):
            copy.wait_send()


def finish_kernel(rows, ret_recv, stat_recv, vout, aout, merged_buf, w_buf, sem):
    rows_out = pltpu.make_async_copy(rows, vout, sem.at[0])
    rows_out.start()
    tiles = []
    for s in range(NC):
        tile = stat_recv[s]
        shift = (128 - 32 * (s % 4)) % 128
        tiles.append(pltpu.roll(tile, shift, 1) if shift else tile)
    peak = tiles[0]
    for tile in tiles[1:]:
        peak = jnp.maximum(peak, tile)
    norm = None
    weights = []
    for tile in tiles:
        w = jnp.exp2((tile - peak) * LOG2E)
        weights.append(w)
        part = w * pltpu.roll(tile, 4, 0)
        norm = part if norm is None else norm + part
    for s in range(NC):
        w_buf[s] = weights[s] / norm
    turned = w_buf[...].reshape(NC * 8, 128).T[:AROWS]
    lane = lax.broadcasted_iota(jnp.int32, (AROWS, 128), 1)
    for pair in range(2):
        lanes = slice(pair * 128, pair * 128 + 128)
        merged = None
        for s in range(NC):
            at = s * 8 + 2 * pair
            w = jnp.where(lane < HEAD_DIM, turned[:, at:at + 1], turned[:, at + 1:at + 2])
            part = w * ret_recv[s, :, lanes].astype(F32)
            merged = part if merged is None else merged + part
        merged_buf[:, lanes] = merged.astype(BF16)
    merged_out = pltpu.make_async_copy(merged_buf, aout, sem.at[1])
    merged_out.start()
    merged_out.wait()
    rows_out.wait()


def shards(video_q, video_k, video_v, audio_q, audio_k, audio_v, norm_gain):
    arrays = (video_q, video_k, video_v, audio_q, audio_k, audio_v, norm_gain.reshape(1, -1))
    arrays = [pltpu.with_memory_space_constraint(a, pltpu.HBM) for a in arrays]
    vmem = pl.BlockSpec(memory_space=pltpu.VMEM)
    dma = pltpu.SemaphoreType.DMA
    rows, ret_recv, stat_recv = pl.pallas_call(
        kernel,
        out_shape=(
            jax.ShapeDtypeStruct((PIECE, NZ * WIDTH), BF16),
            jax.ShapeDtypeStruct((NC, AROWS, WIDTH), BF16),
            jax.ShapeDtypeStruct((NC, 8, 128), F32),
        ),
        in_specs=[pl.BlockSpec(memory_space=pltpu.HBM)] * 7,
        out_specs=(vmem, vmem, vmem),
        scratch_shapes=[
            pltpu.VMEM((1, NZ * WIDTH), F32),
            pltpu.VMEM((ROWS, WIDTH), BF16),
            pltpu.VMEM((ROWS, WIDTH), BF16),
            pltpu.VMEM((ROWS, WIDTH), BF16),
            pltpu.VMEM((4, WIDTH, 256), BF16),
            pltpu.VMEM((4, HEAD_DIM, ROWS), BF16),
            pltpu.VMEM((2, 2 * NC, 2, AROWS, 128), BF16),
            pltpu.VMEM((2 * NC, AROWS, WIDTH), BF16),
            pltpu.VMEM((4, HEAD_DIM, KEYS), BF16),
            pltpu.VMEM((4, WIDTH, 256), BF16),
            pltpu.VMEM((KEYS, 256), F32),
            pltpu.VMEM((KEYS, 256), F32),
            pltpu.VMEM((ROWS, 256), F32),
            pltpu.VMEM((ROWS, 256), F32),
            pltpu.VMEM((WIDTH, 256), F32),
            pltpu.VMEM((2, NZ, PIECE, 128), BF16),
            pltpu.VMEM((2, NZ, PIECE, 128), BF16),
            pltpu.VMEM((2, WIDTH, 256), BF16),
            pltpu.VMEM((2, 8, 256), F32),
            pltpu.VMEM((2, WIDTH, 256), BF16),
            pltpu.VMEM((2, 8, 256), F32),
            pltpu.VMEM((NC, AROWS, WIDTH), BF16),
            pltpu.VMEM((4, 8, 128), F32),
            dma((9,)), dma((2, NC)), dma((2, NC)), dma((NC,)), dma((NC,)), dma((2, 4)), dma((2, 4)),
            dma, dma, dma((2, NZ)), dma((2, NZ)), dma((2,)), dma((2,)), dma((2,)), dma((2,)),
            dma((NC,)), dma((NC,)), dma((NC,)), dma((NC,)),
        ],
        compiler_params=pltpu.CompilerParams(
            collective_id=0, has_side_effects=True, vmem_limit_bytes=24 * 1024 * 1024),
    )(*arrays)
    return pl.pallas_call(
        finish_kernel,
        out_shape=(
            jax.ShapeDtypeStruct((PIECE, NZ * WIDTH), BF16),
            jax.ShapeDtypeStruct((AROWS, WIDTH), BF16),
        ),
        in_specs=[vmem] * 3,
        out_specs=(pl.BlockSpec(memory_space=pltpu.HBM),) * 2,
        scratch_shapes=[
            pltpu.VMEM((AROWS, WIDTH), BF16),
            pltpu.VMEM((NC, 8, 128), F32),
            dma((2,)),
        ],
        compiler_params=pltpu.CompilerParams(vmem_limit_bytes=4 * 1024 * 1024),
    )(rows, ret_recv, stat_recv)


def solution(mesh):
    placed = P("tok", "head")
    return jax.shard_map(
        shards,
        mesh=mesh,
        in_specs=(placed,) * 6 + (P(),),
        out_specs=(P(("tok", "head"), None), placed),
        check_vma=False,
    )
```
